32 devices in a mesh: seq: 8 (over z, x), dp: 4 (over y, core), grp: 1.
Axes of the slice: x: 2, y: 2, z: 4, core: 2. Of those that a mesh axis runs over, the one named last changes fastest.
Arguments:
- video_queries: bfloat16 [4, 1024, 4096], P('dp', 'seq', 'grp'), may hold values from -13.5 to 13.5
- caption_keys: bfloat16 [4, 512, 4096], P('dp', 'seq', 'grp'), may hold values from -6 to 6
- caption_values: bfloat16 [4, 512, 4096], P('dp', 'seq', 'grp'), may hold values from -6 to 6
- out_grad: bfloat16 [4, 1024, 4096], P('dp', 'seq', 'grp'), may hold values from -6 to 6
- head_gate: float32 [32], replicated, may hold values from 0.25 to 2
- video_len: int32 [4], P('dp'), may hold values from 1 to 1024, 2048 in all
- cap_len: int32 [4], P('dp'), may hold values from 1 to 512, 1024 in all
Outputs:
- attended: bfloat16 [4, 1024, 4096], P('dp', 'seq', 'grp')
- query_grad: bfloat16 [4, 1024, 4096], P('dp', 'seq', 'grp')
- key_grad: bfloat16 [4, 512, 4096], P('dp', 'seq', 'grp')
- value_grad: bfloat16 [4, 512, 4096], P('dp', 'seq', 'grp')
- gate_grad: float32 [32], replicated
The draws below stay inside these ranges and needn't reach their ends.
All inputs are finite; a program needn't handle non-finite values. No bound on the sum of `video_len` or of `cap_len` on one device may be relied on, other than what follows from the above.
Results may differ from the reference program's by a relative error of at most 0.017.
Values may be sent and summed in bfloat16 or wider, within the bound.
A program may use at most 64 MiB of HBM per device.

```python
import math
import jax
import jax.numpy as jnp
import numpy as np
from jax import lax

HEADS = 32
HEAD_DIM = 128
TOK_DEV = 128
CAP = 512
INNER = 4096
SAMPLES = 4
VIDEO = 1024
N_SEQ = 8


def paired_fields(key):
    base = jax.random.fold_in(key, 7001)
    width = HEADS * HEAD_DIM
    cap_keys = jnp.clip(jax.random.normal(jax.random.fold_in(base, 1), (SAMPLES, CAP, width), jnp.float32), -6.0, 6.0)
    queries = jnp.clip(jax.random.normal(jax.random.fold_in(base, 2), (SAMPLES, VIDEO, width), jnp.float32), -6.0, 6.0)
    return (queries, cap_keys)


def draw_video_queries(key, part):
    return paired_fields(key)[0].astype(jnp.bfloat16)


def draw_caption_keys(key, part):
    return paired_fields(key)[1].astype(jnp.bfloat16)


def shard_levels(key, extent, split, smallest, top_value):
    factor_of = 1.0
    for axis_at, shards_of in split:
        draws = jax.random.uniform(jax.random.fold_in(jax.random.fold_in(key, 6), axis_at), (shards_of,), jnp.float32, smallest / len(split), top_value / len(split))
        factor_of = factor_of * jnp.repeat(jnp.exp(draws), extent[axis_at] // shards_of).reshape((-1,) + (1,) * (len(extent) - 1 - axis_at))
    return factor_of


def split_up(amount, total, reach, skew):
    portions = [(1 << 20) // math.isqrt(rank ** skew) + 1 for rank in range(2, amount + 1)]
    spare, given = total - reach - (amount - 1), [1] * (amount - 1)
    while spare > 0:
        candidates = [i for i in range(amount - 1) if given[i] < reach]
        whole, budget = sum([portions[i] for i in candidates]), spare
        for i in candidates:
            more = min(reach - given[i], max(1, budget * portions[i] // whole), spare)
            given[i] = given[i] + more
            spare = spare - more
    return np.array([reach] + given)


def uneven_parts(own_key, amount, total, bound, lean):
    if amount == 2:
        one = jax.random.randint(own_key, (), max(1, total - bound), min(bound, total - 1) + 1)
        return jnp.stack([one, total - one])
    lengths = jnp.asarray(split_up(amount, total, bound, lean), jnp.int32)
    twos = (amount - 1) // 2
    source_of, taker = lengths[1:1 + 2 * twos:2], lengths[2:2 + 2 * twos:2]
    slack = jnp.minimum(source_of - 1, bound - taker)
    moved = jax.random.randint(jax.random.fold_in(own_key, 1), (twos,), 0, 1 << 20) % (slack + 1)
    lengths = lengths.at[1:1 + 2 * twos:2].set(source_of - moved).at[2:2 + 2 * twos:2].set(taker + moved)
    return lengths[jax.random.permutation(jax.random.fold_in(own_key, 2), amount)]


def centred(stream_key, extent, spread, bound, pieces=(), held_as=jnp.bfloat16):
    loudness = shard_levels(stream_key, extent, pieces, -0.22, 0.18) if pieces else 1.0
    values = jax.random.normal(stream_key, extent, jnp.float32) * spread * loudness
    return jnp.minimum(jnp.maximum(values, -bound), bound).astype(held_as)


def setup_inputs(seed: int = 0) -> dict:
    splits = jax.random.split(jax.random.key(seed), 8)
    video_queries = draw_video_queries(jax.random.fold_in(splits[7], 71), 0)
    caption_keys = draw_caption_keys(jax.random.fold_in(splits[7], 71), 0)
    caption_values = centred(splits[2], (SAMPLES, CAP, INNER), 1.0, 6.0, ((0, 4), (1, 8)))
    out_grad = centred(splits[3], (SAMPLES, VIDEO, INNER), 1.0, 6.0, ((0, 4), (1, 8)))
    head_gate = jnp.clip(jnp.exp(jax.random.uniform(splits[4], (HEADS,), jnp.float32, math.log(0.25), math.log(2.0))), 0.25, 2.0)
    video_len = uneven_parts(splits[5], SAMPLES, SAMPLES * VIDEO // 2, VIDEO, 2).astype(jnp.int32)
    cap_len = uneven_parts(splits[6], SAMPLES, SAMPLES * CAP // 2, CAP, 1).astype(jnp.int32)
    return dict(video_queries=video_queries, caption_keys=caption_keys, caption_values=caption_values, out_grad=out_grad, head_gate=head_gate, video_len=video_len, cap_len=cap_len)


def split_heads(block):
    return block.reshape(block.shape[0], HEADS, HEAD_DIM)


def rounded(value):
    return lax.optimization_barrier(value.astype(jnp.bfloat16)).astype(jnp.float32)


def reference(video_queries, caption_keys, caption_values, out_grad, head_gate, video_len, cap_len):
    score_scale = HEAD_DIM ** -0.5
    cycle_size = N_SEQ

    def one_sample(packed):
        queries, cap_keys, values, cotangent, vid_length, cap_length = packed
        query_heads = split_heads(queries).astype(jnp.float32)
        key_heads = split_heads(cap_keys).astype(jnp.float32)
        value_heads = split_heads(values).astype(jnp.float32)
        scores = jnp.einsum("thd,jhd->htj", query_heads, key_heads) * score_scale
        key_live = jnp.arange(CAP, dtype=jnp.int32) < cap_length
        scores = jnp.where(key_live[None, None, :], scores, -jnp.inf)
        shifted = jnp.exp(scores - jnp.max(scores, axis=-1, keepdims=True))
        weights = shifted / jnp.sum(shifted, axis=-1, keepdims=True)
        weights_low = rounded(weights)
        attention = jnp.einsum("htj,jhd->thd", weights_low, value_heads)
        row_live = (jnp.arange(VIDEO, dtype=jnp.int32) < vid_length).astype(jnp.float32)[:, None, None]
        head_scale = head_gate.astype(jnp.float32)[None, :, None]
        attended = (attention * head_scale * row_live).astype(jnp.bfloat16).reshape(VIDEO, HEADS * HEAD_DIM)
        cot_heads = split_heads(cotangent).astype(jnp.float32)
        gate_term = jnp.sum(cot_heads * attention * row_live, axis=(0, 2))
        grad_attention = rounded(cot_heads * head_scale * row_live)
        grad_weights = jnp.einsum("thd,jhd->htj", grad_attention, value_heads)
        row_delta = jnp.sum(weights * grad_weights, axis=-1, keepdims=True)
        grad_scores = rounded(weights * (grad_weights - row_delta) * score_scale)
        query_grad = jnp.einsum("htj,jhd->thd", grad_scores, key_heads)
        query_grad = query_grad.astype(jnp.bfloat16).reshape(VIDEO, HEADS * HEAD_DIM)
        block_scores = grad_scores.reshape(HEADS, cycle_size, TOK_DEV, CAP)
        block_weights = weights_low.reshape(HEADS, cycle_size, TOK_DEV, CAP)
        block_queries = query_heads.reshape(cycle_size, TOK_DEV, HEADS, HEAD_DIM)
        block_grads = grad_attention.reshape(cycle_size, TOK_DEV, HEADS, HEAD_DIM)
        key_parts = rounded(jnp.einsum("hrtj,rthd->rjhd", block_scores, block_queries))
        value_parts = rounded(jnp.einsum("hrtj,rthd->rjhd", block_weights, block_grads))
        key_grad = jnp.sum(key_parts, axis=0).astype(jnp.bfloat16).reshape(CAP, HEADS * HEAD_DIM)
        value_grad = jnp.sum(value_parts, axis=0).astype(jnp.bfloat16).reshape(CAP, HEADS * HEAD_DIM)
        return attended, query_grad, key_grad, value_grad, gate_term

    per_sample = lax.map(one_sample, (video_queries, caption_keys, caption_values, out_grad, video_len, cap_len))
    return per_sample[0], per_sample[1], per_sample[2], per_sample[3], jnp.sum(per_sample[4], axis=0)
```

```python
import functools

import jax
import jax.numpy as jnp
from jax import lax
from jax.experimental import pallas as pl
from jax.experimental.pallas import tpu as pltpu
from jax.sharding import PartitionSpec as P

MESH = pl.DeviceIdType.MESH
LANES = 128


def kernel(
    dims,
    gate_ref,
    vlen_ref,
    clen_ref,
    q_ref,
    k_ref,
    v_ref,
    g_ref,
    att_out,
    dq_out,
    dk_out,
    dv_out,
    gate_out,
    qbuf,
    gbuf,
    kbuf,
    vbuf,
    obuf,
    dqbuf,
    dkbuf,
    dvbuf,
    dkpart,
    dvpart,
    gate_seq,
    gate_all,
    gate_mine,
    in_recv,
    in_send,
    out_recv,
    out_send,
    gate_recv,
    gate_send,
):
    n, reps, dp_n, grp_n, heads, block = dims
    size = n // reps
    chunks, _, toks, cw = qbuf.shape
    caps = kbuf.shape[2]
    cols = q_ref.shape[1] // size
    hd = q_ref.shape[1] // heads
    per_chunk = cw // hd
    total_j = n * caps
    total_t = size * toks
    peers = dp_n * grp_n

    me = lax.axis_index("seq")
    dp_me = lax.axis_index("dp")
    grp_me = lax.axis_index("grp")
    half = me // size
    within = lax.rem(me, size)
    side = dp_me * grp_n + grp_me

    barrier = pltpu.get_barrier_semaphore()
    for d in range(1, n):
        pl.semaphore_signal(
            barrier, inc=1, device_id={"seq": lax.rem(me + d, n)}, device_id_type=MESH
        )

    def side_id(d):
        other = lax.rem(side + d, peers)
        return {"dp": other // grp_n, "grp": lax.rem(other, grp_n)}

    def greet(d, carry):
        pl.semaphore_signal(barrier, inc=1, device_id=side_id(d), device_id_type=MESH)
        return carry

    lax.fori_loop(1, peers, greet, 0)
    pl.semaphore_wait(barrier, n - 1 + peers - 1)

    def columns(owner, c):
        return pl.ds(pl.multiple_of(owner * cols + c * cw, LANES), cw)

    def send_in(c, carry):
        for d in range(1, n):
            peer = lax.rem(me + d, n)
            owner = lax.rem(peer, size)
            for kind, (src, dst) in enumerate(((k_ref, kbuf), (v_ref, vbuf))):
                pltpu.make_async_remote_copy(
                    src_ref=src.at[:, columns(owner, c)],
                    dst_ref=dst.at[c, me],
                    send_sem=in_send.at[kind],
                    recv_sem=in_recv.at[kind, c],
                    device_id={"seq": peer},
                    device_id_type=MESH,
                ).start()
            if d < size:
                owner = lax.rem(within + d, size)
                for kind, (src, dst) in enumerate(((q_ref, qbuf), (g_ref, gbuf))):
                    pltpu.make_async_remote_copy(
                        src_ref=src.at[:, columns(owner, c)],
                        dst_ref=dst.at[c, within],
                        send_sem=in_send.at[2 + kind],
                        recv_sem=in_recv.at[2 + kind, c],
                        device_id={"seq": half * size + owner},
                        device_id_type=MESH,
                    ).start()
        for kind, (src, dst, slot) in enumerate(
            ((k_ref, kbuf, me), (v_ref, vbuf, me), (q_ref, qbuf, within), (g_ref, gbuf, within))
        ):
            pltpu.make_async_copy(
                src.at[:, columns(within, c)], dst.at[c, slot], in_recv.at[kind, c]
            ).start()
        return carry

    lax.fori_loop(0, chunks, send_in, 0)

    gate_mine[...] = jnp.zeros_like(gate_mine)
    cap_len = clen_ref[0]
    video_len = vlen_ref[0]
    scale = hd ** (-0.5)
    lane = lax.broadcasted_iota(jnp.int32, gate_mine.shape, 1)

    def transposed(a, b, left, right):
        return lax.dot_general(
            a, b, (((left,), (right,)), ((), ())), preferred_element_type=jnp.float32
        )

    def one_chunk(c, carry):
        for kind, buf in enumerate((kbuf, vbuf, qbuf, gbuf)):
            pltpu.make_async_copy(buf.at[c], buf.at[c], in_recv.at[kind, c]).wait()
        for h in range(per_chunk):
            at = slice(h * hd, (h + 1) * hd)
            head = grp_me * heads + within * (heads // size) + c * per_chunk + h
            gate = gate_ref[head]
            keys = kbuf[c, :, :, at].reshape(total_j, hd)
            values = vbuf[c, :, :, at].reshape(total_j, hd)
            step = block // toks
            dk = jnp.zeros((total_j, hd), jnp.float32)
            dv = jnp.zeros((total_j, hd), jnp.float32)
            gate_sum = jnp.zeros((1, hd), jnp.float32)
            for b in range(total_t // block):
                rows = slice(b * step, (b + 1) * step)
                queries = qbuf[c, rows, :, at].reshape(block, hd)
                cot = gbuf[c, rows, :, at].reshape(block, hd).astype(jnp.float32)
                key_live = lax.broadcasted_iota(jnp.int32, (total_j, block), 0) < cap_len
                scores = transposed(keys, queries, 1, 1) * scale
                scores = jnp.where(key_live, scores, -jnp.inf)
                shifted = jnp.exp(scores - jnp.max(scores, axis=0, keepdims=True))
                weights = shifted * (1.0 / jnp.sum(shifted, axis=0, keepdims=True))
                low = weights.astype(jnp.bfloat16)
                attention = transposed(values, low, 0, 0).T
                first = half * total_t + b * block
                row = first + lax.broadcasted_iota(jnp.int32, (block, hd), 0)
                live = (row < video_len).astype(jnp.float32)
                obuf[c, rows, :, at] = (
                    (attention * gate * live).astype(jnp.bfloat16).reshape(step, toks, hd)
                )
                gate_sum += jnp.sum(cot * attention * live, axis=0, keepdims=True)
                grad = (cot * gate * live).astype(jnp.bfloat16)
                gw = transposed(values, grad, 1, 1)
                delta = jnp.sum(weights * gw, axis=0, keepdims=True)
                gs = (weights * (gw - delta) * scale).astype(jnp.bfloat16)
                dq = transposed(keys, gs, 0, 0).T
                dqbuf[c, rows, :, at] = dq.astype(jnp.bfloat16).reshape(step, toks, hd)
                dk += jnp.dot(gs, queries, preferred_element_type=jnp.float32)
                dv += jnp.dot(low, grad, preferred_element_type=jnp.float32)
            dkbuf[c, :, :, at] = dk.astype(jnp.bfloat16).reshape(n, caps, hd)
            dvbuf[c, :, :, at] = dv.astype(jnp.bfloat16).reshape(n, caps, hd)
            gate_mine[...] += jnp.where(
                lane == head, jnp.sum(gate_sum, axis=1, keepdims=True), 0.0
            )
        mine = columns(within, c)
        for d in range(1, n):
            peer = lax.rem(me + d, n)
            for kind, (src, dst) in enumerate(((dkbuf, dkpart), (dvbuf, dvpart))):
                pltpu.make_async_remote_copy(
                    src_ref=src.at[c, peer],
                    dst_ref=dst.at[half, :, mine],
                    send_sem=out_send.at[kind],
                    recv_sem=out_recv.at[kind],
                    device_id={"seq": peer},
                    device_id_type=MESH,
                ).start()
            if d < size:
                owner = lax.rem(within + d, size)
                for kind, (src, dst) in enumerate(((obuf, att_out), (dqbuf, dq_out))):
                    pltpu.make_async_remote_copy(
                        src_ref=src.at[c, owner],
                        dst_ref=dst.at[:, mine],
                        send_sem=out_send.at[2 + kind],
                        recv_sem=out_recv.at[2 + kind],
                        device_id={"seq": half * size + owner},
                        device_id_type=MESH,
                    ).start()
        for kind, (src, dst) in enumerate(
            (
                (dkbuf.at[c, me], dkpart.at[half, :, mine]),
                (dvbuf.at[c, me], dvpart.at[half, :, mine]),
                (obuf.at[c, within], att_out.at[:, mine]),
                (dqbuf.at[c, within], dq_out.at[:, mine]),
            )
        ):
            pltpu.make_async_copy(src, dst, out_recv.at[kind]).start()
        return carry

    lax.fori_loop(0, chunks, one_chunk, 0)

    def send_gate(src, dst, count, slot, stage, target):
        pltpu.make_async_copy(src, dst.at[slot], gate_recv.at[stage]).start()

        def go(d, carry):
            pltpu.make_async_remote_copy(
                src_ref=src,
                dst_ref=dst.at[slot],
                send_sem=gate_send.at[stage],
                recv_sem=gate_recv.at[stage],
                device_id=target(d),
                device_id_type=MESH,
            ).start()
            return carry

        lax.fori_loop(1, count, go, 0)
        pltpu.make_async_copy(dst, dst, gate_recv.at[stage]).wait()
        if count > 1:
            sent = dst.at[pl.ds(0, count - 1)]
            pltpu.make_async_copy(sent, sent, gate_send.at[stage]).wait()

    send_gate(gate_mine, gate_seq, n, me, 0, lambda d: {"seq": lax.rem(me + d, n)})
    gate_mine[...] = jnp.sum(gate_seq[...], axis=0)
    send_gate(gate_mine, gate_all, peers, side, 1, side_id)
    gate_out[...] = jnp.sum(gate_all[...], axis=0)

    for kind, ref in enumerate((dkpart, dvpart, att_out, dq_out)):
        pltpu.make_async_copy(ref, ref, out_recv.at[kind]).wait()
    dk_out[...] = jnp.sum(dkpart[...].astype(jnp.float32), axis=0).astype(jnp.bfloat16)
    dv_out[...] = jnp.sum(dvpart[...].astype(jnp.float32), axis=0).astype(jnp.bfloat16)
    for kind, (ins, outs) in enumerate(
        ((kbuf, dkbuf), (vbuf, dvbuf), (qbuf, obuf), (gbuf, dqbuf))
    ):
        count = (n if kind < 2 else size) - 1
        if count > 0:
            sent = ins.at[:, pl.ds(0, count)]
            pltpu.make_async_copy(sent, sent, in_send.at[kind]).wait()
            sent = outs.at[:, pl.ds(0, count)]
            pltpu.make_async_copy(sent, sent, out_send.at[kind]).wait()


def per_device(mesh_shape, video_queries, caption_keys, caption_values, out_grad, head_gate, video_len, cap_len):
    n, dp_n, grp_n = mesh_shape["seq"], mesh_shape["dp"], mesh_shape["grp"]
    toks, width = video_queries.shape[1:]
    caps = caption_keys.shape[1]
    head_count = head_gate.shape[0]
    heads = head_count // grp_n
    reps = 2 if n % 2 == 0 and heads % (n // 2) == 0 else 1
    size = n // reps
    cols = width // size
    own_heads = heads // size
    chunks = 4 if own_heads % 4 == 0 else own_heads
    cw = cols // chunks
    block = toks * 2 if size % 2 == 0 else toks
    lanes = -(-head_count // LANES) * LANES
    low = jnp.bfloat16
    any_spec = pl.BlockSpec(memory_space=pl.ANY)
    smem = pl.BlockSpec(memory_space=pltpu.SMEM)
    vmem = pl.BlockSpec(memory_space=pltpu.VMEM)
    out = pl.pallas_call(
        functools.partial(kernel, (n, reps, dp_n, grp_n, heads, block)),
        out_shape=(
            jax.ShapeDtypeStruct((toks, width), low),
            jax.ShapeDtypeStruct((toks, width), low),
            jax.ShapeDtypeStruct((caps, width), low),
            jax.ShapeDtypeStruct((caps, width), low),
            jax.ShapeDtypeStruct((8, lanes), jnp.float32),
        ),
        in_specs=[smem, smem, smem, any_spec, any_spec, any_spec, any_spec],
        out_specs=(any_spec, any_spec, vmem, vmem, vmem),
        scratch_shapes=[
            pltpu.VMEM((chunks, size, toks, cw), low),
            pltpu.VMEM((chunks, size, toks, cw), low),
            pltpu.VMEM((chunks, n, caps, cw), low),
            pltpu.VMEM((chunks, n, caps, cw), low),
            pltpu.VMEM((chunks, size, toks, cw), low),
            pltpu.VMEM((chunks, size, toks, cw), low),
            pltpu.VMEM((chunks, n, caps, cw), low),
            pltpu.VMEM((chunks, n, caps, cw), low),
            pltpu.VMEM((reps, caps, width), low),
            pltpu.VMEM((reps, caps, width), low),
            pltpu.VMEM((n, 8, lanes), jnp.float32),
            pltpu.VMEM((dp_n * grp_n, 8, lanes), jnp.float32),
            pltpu.VMEM((8, lanes), jnp.float32),
            pltpu.SemaphoreType.DMA((4, chunks)),
            pltpu.SemaphoreType.DMA((4,)),
            pltpu.SemaphoreType.DMA((4,)),
            pltpu.SemaphoreType.DMA((4,)),
            pltpu.SemaphoreType.DMA((2,)),
            pltpu.SemaphoreType.DMA((2,)),
        ],
        compiler_params=pltpu.CompilerParams(collective_id=0, has_side_effects=True),
    )(
        head_gate,
        video_len,
        cap_len,
        video_queries[0],
        caption_keys[0],
        caption_values[0],
        out_grad[0],
    )
    gate_grad = out[4][0, :head_count]
    return (out[0][None], out[1][None], out[2][None], out[3][None], gate_grad)


def solution(mesh):
    rows = P("dp", "seq", "grp")
    return jax.shard_map(
        functools.partial(per_device, dict(mesh.shape)),
        mesh=mesh,
        in_specs=(rows, rows, rows, rows, P(), P("dp"), P("dp")),
        out_specs=(rows, rows, rows, rows, P()),
        check_vma=False,
    )
```

```python
import functools

import jax
import jax.numpy as jnp
from jax import lax
from jax.experimental import pallas as pl
from jax.experimental.pallas import tpu as pltpu
from jax.sharding import PartitionSpec as P

MESH = pl.DeviceIdType.MESH
LANES = 128
VMEM_LIMIT = 24 << 20


def kernel(
    dims,
    gate_ref,
    vlen_ref,
    clen_ref,
    q_ref,
    k_ref,
    v_ref,
    g_ref,
    att_out,
    dq_out,
    dkpart,
    dvpart,
    gate_out,
    qbuf,
    gbuf,
    kbuf,
    vbuf,
    obuf,
    dqbuf,
    dkbuf,
    dvbuf,
    gate_seq,
    gate_all,
    gate_mine,
    in_recv,
    in_send,
    out_recv,
    out_send,
    gate_recv,
    gate_send,
):
    n, reps, dp_n, grp_n, heads, block = dims
    size = n // reps
    chunks, _, toks, cw = qbuf.shape
    caps = kbuf.shape[2]
    cols = q_ref.shape[1] // size
    hd = q_ref.shape[1] // heads
    per_chunk = cw // hd
    total_j = n * caps
    total_t = size * toks
    peers = dp_n * grp_n

    me = lax.axis_index("seq")
    dp_me = lax.axis_index("dp")
    grp_me = lax.axis_index("grp")
    half = me // size
    within = lax.rem(me, size)
    side = dp_me * grp_n + grp_me

    barrier = pltpu.get_barrier_semaphore()
    for d in range(1, n):
        pl.semaphore_signal(
            barrier, inc=1, device_id={"seq": lax.rem(me + d, n)}, device_id_type=MESH
        )

    def side_id(d):
        other = lax.rem(side + d, peers)
        return {"dp": other // grp_n, "grp": lax.rem(other, grp_n)}

    def greet(d, carry):
        pl.semaphore_signal(barrier, inc=1, device_id=side_id(d), device_id_type=MESH)
        return carry

    lax.fori_loop(1, peers, greet, 0)
    pl.semaphore_wait(barrier, n - 1 + peers - 1)

    def columns(owner, c):
        return pl.ds(pl.multiple_of(owner * cols + c * cw, LANES), cw)

    def send_in(c, carry):
        for d in range(1, n):
            peer = lax.rem(me + d, n)
            owner = lax.rem(peer, size)
            for kind, (src, dst) in enumerate(((k_ref, kbuf), (v_ref, vbuf))):
                pltpu.make_async_remote_copy(
                    src_ref=src.at[:, columns(owner, c)],
                    dst_ref=dst.at[c, me],
                    send_sem=in_send.at[kind],
                    recv_sem=in_recv.at[kind, c],
                    device_id={"seq": peer},
                    device_id_type=MESH,
                ).start()
            if d < size:
                owner = lax.rem(within + d, size)
                for kind, (src, dst) in enumerate(((q_ref, qbuf), (g_ref, gbuf))):
                    pltpu.make_async_remote_copy(
                        src_ref=src.at[:, columns(owner, c)],
                        dst_ref=dst.at[c, within],
                        send_sem=in_send.at[2 + kind],
                        recv_sem=in_recv.at[2 + kind, c],
                        device_id={"seq": half * size + owner},
                        device_id_type=MESH,
                    ).start()
        for kind, (src, dst, slot) in enumerate(
            ((k_ref, kbuf, me), (v_ref, vbuf, me), (q_ref, qbuf, within), (g_ref, gbuf, within))
        ):
            pltpu.make_async_copy(
                src.at[:, columns(within, c)], dst.at[c, slot], in_recv.at[kind, c]
            ).start()
        return carry

    lax.fori_loop(0, chunks, send_in, 0)

    gate_mine[...] = jnp.zeros_like(gate_mine)
    cap_len = clen_ref[0]
    video_len = vlen_ref[0]
    scale = hd ** (-0.5)
    lane = lax.broadcasted_iota(jnp.int32, gate_mine.shape, 1)

    def transposed(a, b, left, right):
        return lax.dot_general(
            a, b, (((left,), (right,)), ((), ())), preferred_element_type=jnp.float32
        )

    def one_chunk(c, carry):
        for kind, buf in enumerate((kbuf, vbuf, qbuf, gbuf)):
            pltpu.make_async_copy(buf.at[c], buf.at[c], in_recv.at[kind, c]).wait()
        for h in range(per_chunk):
            at = slice(h * hd, (h + 1) * hd)
            head = grp_me * heads + within * (heads // size) + c * per_chunk + h
            gate = gate_ref[head]
            keys = kbuf[c, :, :, at].reshape(total_j, hd)
            values = vbuf[c, :, :, at].reshape(total_j, hd)
            step = block // toks
            dk = jnp.zeros((total_j, hd), jnp.float32)
            dv = jnp.zeros((total_j, hd), jnp.float32)
            gate_sum = jnp.zeros((1, hd), jnp.float32)
            for b in range(total_t // block):
                rows = slice(b * step, (b + 1) * step)
                queries = qbuf[c, rows, :, at].reshape(block, hd)
                cot = gbuf[c, rows, :, at].reshape(block, hd).astype(jnp.float32)
                key_live = lax.broadcasted_iota(jnp.int32, (total_j, block), 0) < cap_len
                scores = transposed(keys, queries, 1, 1) * scale
                scores = jnp.where(key_live, scores, -jnp.inf)
                shifted = jnp.exp(scores - jnp.max(scores, axis=0, keepdims=True))
                weights = shifted * (1.0 / jnp.sum(shifted, axis=0, keepdims=True))
                low = weights.astype(jnp.bfloat16)
                attention = transposed(values, low, 0, 0).T
                first = half * total_t + b * block
                row = first + lax.broadcasted_iota(jnp.int32, (block, hd), 0)
                live = (row < video_len).astype(jnp.float32)
                obuf[c, rows, :, at] = (
                    (attention * gate * live).astype(jnp.bfloat16).reshape(step, toks, hd)
                )
                gate_sum += jnp.sum(cot * attention * live, axis=0, keepdims=True)
                grad = (cot * gate * live).astype(jnp.bfloat16)
                gw = transposed(values, grad, 1, 1)
                delta = jnp.sum(weights * gw, axis=0, keepdims=True)
                gs = (weights * (gw - delta) * scale).astype(jnp.bfloat16)
                dq = transposed(keys, gs, 0, 0).T
                dqbuf[c, rows, :, at] = dq.astype(jnp.bfloat16).reshape(step, toks, hd)
                dk += jnp.dot(gs, queries, preferred_element_type=jnp.float32)
                dv += jnp.dot(low, grad, preferred_element_type=jnp.float32)
            dkbuf[c, :, :, at] = dk.astype(jnp.bfloat16).reshape(n, caps, hd)
            dvbuf[c, :, :, at] = dv.astype(jnp.bfloat16).reshape(n, caps, hd)
            gate_mine[...] += jnp.where(
                lane == head, jnp.sum(gate_sum, axis=1, keepdims=True), 0.0
            )
        mine = columns(within, c)
        for d in range(1, n):
            peer = lax.rem(me + d, n)
            for kind, (src, dst) in enumerate(((dkbuf, dkpart), (dvbuf, dvpart))):
                pltpu.make_async_remote_copy(
                    src_ref=src.at[c, peer],
                    dst_ref=dst.at[half, :, mine],
                    send_sem=out_send.at[kind],
                    recv_sem=out_recv.at[kind],
                    device_id={"seq": peer},
                    device_id_type=MESH,
                ).start()
            if d < size:
                owner = lax.rem(within + d, size)
                for kind, (src, dst) in enumerate(((obuf, att_out), (dqbuf, dq_out))):
                    pltpu.make_async_remote_copy(
                        src_ref=src.at[c, owner],
                        dst_ref=dst.at[:, mine],
                        send_sem=out_send.at[2 + kind],
                        recv_sem=out_recv.at[2 + kind],
                        device_id={"seq": half * size + owner},
                        device_id_type=MESH,
                    ).start()
        for kind, (src, dst) in enumerate(
            (
                (dkbuf.at[c, me], dkpart.at[half, :, mine]),
                (dvbuf.at[c, me], dvpart.at[half, :, mine]),
                (obuf.at[c, within], att_out.at[:, mine]),
                (dqbuf.at[c, within], dq_out.at[:, mine]),
            )
        ):
            pltpu.make_async_copy(src, dst, out_recv.at[kind]).start()
        return carry

    lax.fori_loop(0, chunks, one_chunk, 0)

    def send_gate(src, dst, count, slot, stage, target):
        pltpu.make_async_copy(src, dst.at[slot], gate_recv.at[stage]).start()

        def go(d, carry):
            pltpu.make_async_remote_copy(
                src_ref=src,
                dst_ref=dst.at[slot],
                send_sem=gate_send.at[stage],
                recv_sem=gate_recv.at[stage],
                device_id=target(d),
                device_id_type=MESH,
            ).start()
            return carry

        lax.fori_loop(1, count, go, 0)
        pltpu.make_async_copy(dst, dst, gate_recv.at[stage]).wait()
        if count > 1:
            sent = dst.at[pl.ds(0, count - 1)]
            pltpu.make_async_copy(sent, sent, gate_send.at[stage]).wait()

    send_gate(gate_mine, gate_seq, n, me, 0, lambda d: {"seq": lax.rem(me + d, n)})
    gate_mine[...] = jnp.sum(gate_seq[...], axis=0)
    send_gate(gate_mine, gate_all, peers, side, 1, side_id)
    gate_out[...] = jnp.sum(gate_all[...], axis=0)

    for kind, ref in enumerate((dkpart, dvpart, att_out, dq_out)):
        pltpu.make_async_copy(ref, ref, out_recv.at[kind]).wait()
    for kind, (ins, outs) in enumerate(
        ((kbuf, dkbuf), (vbuf, dvbuf), (qbuf, obuf), (gbuf, dqbuf))
    ):
        count = (n if kind < 2 else size) - 1
        if count > 0:
            sent = ins.at[:, pl.ds(0, count)]
            pltpu.make_async_copy(sent, sent, in_send.at[kind]).wait()
            sent = outs.at[:, pl.ds(0, count)]
            pltpu.make_async_copy(sent, sent, out_send.at[kind]).wait()


def land_kernel(att, dq, dk, dv, gate, att_out, dq_out, dk_out, dv_out, gate_out):
    att_out[0] = att[...]
    dq_out[0] = dq[...]
    dk_out[0] = jnp.sum(dk[...].astype(jnp.float32), axis=0).astype(dk_out.dtype)
    dv_out[0] = jnp.sum(dv[...].astype(jnp.float32), axis=0).astype(dv_out.dtype)
    gate_out[...] = gate[:1, : gate_out.shape[1]]


def land(parts, head_count):
    att, dq, dk, dv, gate = parts
    (toks, width), (reps, caps, _) = att.shape, dk.shape
    steps = max(1, width // 1024)
    cw = width // steps
    rows = pl.BlockSpec((toks, cw), lambda i: (0, i))
    pieces = pl.BlockSpec((reps, caps, cw), lambda i: (0, 0, i))
    token = pl.BlockSpec((1, toks, cw), lambda i: (0, 0, i))
    cap = pl.BlockSpec((1, caps, cw), lambda i: (0, 0, i))
    out = pl.pallas_call(
        land_kernel,
        grid=(steps,),
        out_shape=(
            jax.ShapeDtypeStruct((1, toks, width), att.dtype),
            jax.ShapeDtypeStruct((1, toks, width), dq.dtype),
            jax.ShapeDtypeStruct((1, caps, width), dk.dtype),
            jax.ShapeDtypeStruct((1, caps, width), dv.dtype),
            jax.ShapeDtypeStruct((1, head_count), gate.dtype),
        ),
        in_specs=[rows, rows, pieces, pieces, pl.BlockSpec(gate.shape, lambda i: (0, 0))],
        out_specs=(token, token, cap, cap, pl.BlockSpec((1, head_count), lambda i: (0, 0))),
        compiler_params=pltpu.CompilerParams(vmem_limit_bytes=VMEM_LIMIT),
    )(att, dq, dk, dv, gate)
    return (*out[:4], out[4][0])


def per_device(mesh_shape, video_queries, caption_keys, caption_values, out_grad, head_gate, video_len, cap_len):
    n, dp_n, grp_n = mesh_shape["seq"], mesh_shape["dp"], mesh_shape["grp"]
    toks, width = video_queries.shape[1:]
    caps = caption_keys.shape[1]
    head_count = head_gate.shape[0]
    heads = head_count // grp_n
    reps = 2 if n % 2 == 0 and heads % (n // 2) == 0 else 1
    size = n // reps
    cols = width // size
    own_heads = heads // size
    chunks = 4 if own_heads % 4 == 0 else own_heads
    cw = cols // chunks
    block = toks * 2 if size % 2 == 0 else toks
    lanes = -(-head_count // LANES) * LANES
    low = jnp.bfloat16
    any_spec = pl.BlockSpec(memory_space=pl.ANY)
    smem = pl.BlockSpec(memory_space=pltpu.SMEM)
    vmem = pl.BlockSpec(memory_space=pltpu.VMEM)
    out = pl.pallas_call(
        functools.partial(kernel, (n, reps, dp_n, grp_n, heads, block)),
        out_shape=(
            jax.ShapeDtypeStruct((toks, width), low),
            jax.ShapeDtypeStruct((toks, width), low),
            jax.ShapeDtypeStruct((reps, caps, width), low),
            jax.ShapeDtypeStruct((reps, caps, width), low),
            jax.ShapeDtypeStruct((8, lanes), jnp.float32),
        ),
        in_specs=[smem, smem, smem, any_spec, any_spec, any_spec, any_spec],
        out_specs=(any_spec, any_spec, any_spec, any_spec, vmem),
        scratch_shapes=[
            pltpu.VMEM((chunks, size, toks, cw), low),
            pltpu.VMEM((chunks, size, toks, cw), low),
            pltpu.VMEM((chunks, n, caps, cw), low),
            pltpu.VMEM((chunks, n, caps, cw), low),
            pltpu.VMEM((chunks, size, toks, cw), low),
            pltpu.VMEM((chunks, size, toks, cw), low),
            pltpu.VMEM((chunks, n, caps, cw), low),
            pltpu.VMEM((chunks, n, caps, cw), low),
            pltpu.VMEM((n, 8, lanes), jnp.float32),
            pltpu.VMEM((dp_n * grp_n, 8, lanes), jnp.float32),
            pltpu.VMEM((8, lanes), jnp.float32),
            pltpu.SemaphoreType.DMA((4, chunks)),
            pltpu.SemaphoreType.DMA((4,)),
            pltpu.SemaphoreType.DMA((4,)),
            pltpu.SemaphoreType.DMA((4,)),
            pltpu.SemaphoreType.DMA((2,)),
            pltpu.SemaphoreType.DMA((2,)),
        ],
        compiler_params=pltpu.CompilerParams(
            collective_id=0, has_side_effects=True, vmem_limit_bytes=VMEM_LIMIT
        ),
    )(
        head_gate,
        video_len,
        cap_len,
        video_queries[0],
        caption_keys[0],
        caption_values[0],
        out_grad[0],
    )
    return land(out, head_count)


def solution(mesh):
    rows = P("dp", "seq", "grp")
    return jax.shard_map(
        functools.partial(per_device, dict(mesh.shape)),
        mesh=mesh,
        in_specs=(rows, rows, rows, rows, P(), P("dp"), P("dp")),
        out_specs=(rows, rows, rows, rows, P()),
        check_vma=False,
    )
```

```python
import functools

import jax
import jax.numpy as jnp
from jax import lax
from jax.experimental import pallas as pl
from jax.experimental.pallas import tpu as pltpu
from jax.sharding import PartitionSpec as P

MESH = pl.DeviceIdType.MESH
LANES = 128
VMEM_LIMIT = 36 << 20


def kernel(
    dims,
    gate_ref,
    vlen_ref,
    clen_ref,
    q_ref,
    k_ref,
    v_ref,
    g_ref,
    att_out,
    dq_out,
    kv_out,
    gate_out,
    qbuf,
    gbuf,
    kvbuf,
    obuf,
    dqbuf,
    part,
    part_up,
    part_down,
    gate_seq,
    gate_all,
    gate_mine,
    kv_recv,
    row_recv,
    pair_send,
    hop_recv,
    hop_send,
    sum_recv,
    sum_send,
    out_recv,
    out_send,
    gate_recv,
    gate_send,
):
    n, pair, dp_n, grp_n, heads = dims
    line = n // pair
    chunks, _, toks, cw = qbuf.shape
    caps = kvbuf.shape[3]
    cols = q_ref.shape[1] // pair
    hd = q_ref.shape[1] // heads
    per_chunk = cw // hd
    total_j = n * caps
    total_t = pair * toks
    peers = dp_n * grp_n
    lags = [0] + [s + 1 for s in range(1, line)]
    lag = lags[-1]

    me = lax.axis_index("seq")
    dp_me = lax.axis_index("dp")
    grp_me = lax.axis_index("grp")
    z = me // pair
    x = lax.rem(me, pair)
    side = dp_me * grp_n + grp_me

    barrier = pltpu.get_barrier_semaphore()
    for d in range(1, n):
        pl.semaphore_signal(
            barrier, inc=1, device_id={"seq": lax.rem(me + d, n)}, device_id_type=MESH
        )

    def side_id(d):
        other = lax.rem(side + d, peers)
        return {"dp": other // grp_n, "grp": lax.rem(other, grp_n)}

    def greet(d, carry):
        pl.semaphore_signal(barrier, inc=1, device_id=side_id(d), device_id_type=MESH)
        return carry

    lax.fori_loop(1, peers, greet, 0)
    pl.semaphore_wait(barrier, n - 1 + peers - 1)

    def columns(owner, c):
        return pl.ds(pl.multiple_of(owner * cols + c * cw, LANES), cw)

    def remote(src, dst, send, recv, seq):
        return pltpu.make_async_remote_copy(
            src_ref=src,
            dst_ref=dst,
            send_sem=send,
            recv_sem=recv,
            device_id={"seq": seq},
            device_id_type=MESH,
        )

    def slots(at):
        return pl.ds(at * pair, pair)

    def settle(ref, sem):
        pltpu.make_async_copy(ref, ref, sem).wait()

    def pair_inputs(c, carry):
        pieces = (
            (k_ref, kvbuf.at[c, me, 0], kv_recv.at[c]),
            (v_ref, kvbuf.at[c, me, 1], kv_recv.at[c]),
            (q_ref, qbuf.at[c, x], row_recv.at[0, c]),
            (g_ref, gbuf.at[c, x], row_recv.at[1, c]),
        )
        for d in range(1, pair):
            other = lax.rem(x + d, pair)
            for kind, (src, dst, sem) in enumerate(pieces):
                remote(
                    src.at[:, columns(other, c)], dst, pair_send.at[kind], sem, z * pair + other
                ).start()
        for src, dst, sem in pieces:
            pltpu.make_async_copy(src.at[:, columns(x, c)], dst, sem).start()
        return carry

    lax.fori_loop(0, chunks, pair_inputs, 0)

    gate_mine[...] = jnp.zeros_like(gate_mine)
    cap_len = clen_ref[0]
    video_len = vlen_ref[0]
    scale = hd ** (-0.5)
    lane = lax.broadcasted_iota(jnp.int32, gate_mine.shape, 1)

    def hop_up(c, s):
        block = kvbuf.at[c, slots(z - s)]
        return remote(block, block, hop_send.at[0, s, c], hop_recv.at[0, s + 1, c], me + pair)

    def hop_down(c, s):
        block = kvbuf.at[c, slots(z + s)]
        return remote(block, block, hop_send.at[1, s, c], hop_recv.at[1, s + 1, c], me - pair)

    def goes_up(s):
        return jnp.logical_and(z - s >= 0, z + 1 < line)

    def goes_down(s):
        return jnp.logical_and(z + s < line, z >= 1)

    def relay(c, s):
        if s == 0:
            settle(kvbuf.at[c, slots(z)], kv_recv.at[c])
        else:

            @pl.when(z - s >= 0)
            def _():
                settle(kvbuf.at[c, slots(z - s)], hop_recv.at[0, s, c])

            @pl.when(z + s < line)
            def _():
                settle(kvbuf.at[c, slots(z + s)], hop_recv.at[1, s, c])

        if s < line - 1:

            @pl.when(goes_up(s))
            def _():
                hop_up(c, s).start()

            @pl.when(goes_down(s))
            def _():
                hop_down(c, s).start()

    def transposed(a, b, left, right):
        return lax.dot_general(
            a, b, (((left,), (right,)), ((), ())), preferred_element_type=jnp.float32
        )

    def attend(c):
        settle(qbuf.at[c], row_recv.at[0, c])
        settle(gbuf.at[c], row_recv.at[1, c])
        for h in range(per_chunk):
            at = slice(h * hd, (h + 1) * hd)
            head = grp_me * heads + x * (heads // pair) + c * per_chunk + h
            gate = gate_ref[head]
            keys = kvbuf[c, :, 0, :, at].reshape(total_j, hd)
            values = kvbuf[c, :, 1, :, at].reshape(total_j, hd)
            queries = qbuf[c, :, :, at].reshape(total_t, hd)
            cot = gbuf[c, :, :, at].reshape(total_t, hd).astype(jnp.float32)
            key_live = lax.broadcasted_iota(jnp.int32, (total_j, total_t), 0) < cap_len
            scores = transposed(keys, queries, 1, 1) * scale
            scores = jnp.where(key_live, scores, -jnp.inf)
            shifted = jnp.exp(scores - jnp.max(scores, axis=0, keepdims=True))
            weights = shifted * (1.0 / jnp.sum(shifted, axis=0, keepdims=True))
            low = weights.astype(jnp.bfloat16)
            attention = transposed(values, low, 0, 0).T
            row = z * total_t + lax.broadcasted_iota(jnp.int32, (total_t, hd), 0)
            live = (row < video_len).astype(jnp.float32)
            obuf[c, :, :, at] = (
                (attention * gate * live).astype(jnp.bfloat16).reshape(pair, toks, hd)
            )
            gate_sum = jnp.sum(cot * attention * live, axis=0, keepdims=True)
            grad = (cot * gate * live).astype(jnp.bfloat16)
            gw = transposed(values, grad, 1, 1)
            delta = jnp.sum(weights * gw, axis=0, keepdims=True)
            gs = (weights * (gw - delta) * scale).astype(jnp.bfloat16)
            dq = transposed(keys, gs, 0, 0).T
            dqbuf[c, :, :, at] = dq.astype(jnp.bfloat16).reshape(pair, toks, hd)
            dk = jnp.dot(gs, queries, preferred_element_type=jnp.float32)
            dv = jnp.dot(low, grad, preferred_element_type=jnp.float32)
            part[c, :, 0, :, at] = dk.astype(jnp.bfloat16).reshape(n, caps, hd)
            part[c, :, 1, :, at] = dv.astype(jnp.bfloat16).reshape(n, caps, hd)
            gate_mine[...] += jnp.where(
                lane == head, jnp.sum(gate_sum, axis=1, keepdims=True), 0.0
            )
        mine = columns(x, c)
        for kind, (src, dst) in enumerate(((obuf, att_out), (dqbuf, dq_out))):
            for d in range(1, pair):
                other = lax.rem(x + d, pair)
                remote(
                    src.at[c, other],
                    dst.at[:, mine],
                    out_send.at[kind],
                    out_recv.at[kind],
                    z * pair + other,
                ).start()
            pltpu.make_async_copy(src.at[c, x], dst.at[:, mine], out_recv.at[kind]).start()

    def gather(c, at, way, source):
        settle(source.at[c, slots(at)], sum_recv.at[way, at, c])
        both = part[c, slots(at)].astype(jnp.float32) + source[c, slots(at)].astype(jnp.float32)
        part[c, slots(at)] = both.astype(jnp.bfloat16)

    def sum_up(c, at):
        return remote(
            part.at[c, slots(at)],
            part_up.at[c, slots(at)],
            sum_send.at[0, at, c],
            sum_recv.at[0, at, c],
            me + pair,
        )

    def sum_down(c, at):
        return remote(
            part.at[c, slots(at)],
            part_down.at[c, slots(at)],
            sum_send.at[1, at, c],
            sum_recv.at[1, at, c],
            me - pair,
        )

    def chain_up(c):
        for at in range(line - 1, 0, -1):

            @pl.when(at > z)
            def _():
                @pl.when(z > 0)
                def _():
                    gather(c, at, 0, part_up)

                sum_up(c, at).start()

    def chain_down(c):
        for at in range(line - 1):

            @pl.when(at < z)
            def _():
                @pl.when(z < line - 1)
                def _():
                    gather(c, at, 1, part_down)

                sum_down(c, at).start()

    def finish(c):
        @pl.when(z > 0)
        def _():
            gather(c, z, 0, part_up)

        @pl.when(z < line - 1)
        def _():
            gather(c, z, 1, part_down)

        mine = columns(x, c)
        for d in range(1, pair):
            other = lax.rem(x + d, pair)
            remote(
                part.at[c, z * pair + other],
                kv_out.at[:, :, mine],
                out_send.at[2],
                out_recv.at[2],
                z * pair + other,
            ).start()
        pltpu.make_async_copy(part.at[c, me], kv_out.at[:, :, mine], out_recv.at[2]).start()

    def within(c, run):
        @pl.when(jnp.logical_and(c >= 0, c < chunks))
        def _():
            run(c)

    def step(i, carry):
        for s in range(line):
            within(i - lags[s], functools.partial(relay, s=s))
        within(i - lag, attend)
        within(i - lag - z, chain_up)
        within(i - lag - (line - 1 - z), chain_down)
        within(i - lag - (line - 1), finish)
        return carry

    lax.fori_loop(0, chunks + lag + line - 1, step, 0)

    def send_gate(src, dst, count, slot, stage, target):
        pltpu.make_async_copy(src, dst.at[slot], gate_recv.at[stage]).start()

        def go(d, carry):
            pltpu.make_async_remote_copy(
                src_ref=src,
                dst_ref=dst.at[slot],
                send_sem=gate_send.at[stage],
                recv_sem=gate_recv.at[stage],
                device_id=target(d),
                device_id_type=MESH,
            ).start()
            return carry

        lax.fori_loop(1, count, go, 0)
        settle(dst, gate_recv.at[stage])
        if count > 1:
            settle(dst.at[pl.ds(0, count - 1)], gate_send.at[stage])

    send_gate(gate_mine, gate_seq, n, me, 0, lambda d: {"seq": lax.rem(me + d, n)})
    gate_mine[...] = jnp.sum(gate_seq[...], axis=0)
    send_gate(gate_mine, gate_all, peers, side, 1, side_id)
    gate_out[...] = jnp.sum(gate_all[...], axis=0)

    for kind, ref in enumerate((att_out, dq_out, kv_out)):
        settle(ref, out_recv.at[kind])
    if pair > 1:
        for kind in range(2):
            settle(kvbuf.at[:, pl.ds(0, pair - 1), 0], pair_send.at[kind])
            settle(qbuf.at[:, pl.ds(0, pair - 1)], pair_send.at[2 + kind])
            settle(obuf.at[:, pl.ds(0, pair - 1)], out_send.at[kind])
        settle(kvbuf.at[:, pl.ds(0, pair - 1)], out_send.at[2])

    def drain(c, carry):
        for s in range(line - 1):

            @pl.when(goes_up(s))
            def _():
                hop_up(c, s).wait_send()

            @pl.when(goes_down(s))
            def _():
                hop_down(c, s).wait_send()

        for at in range(line):

            @pl.when(jnp.logical_and(at > z, z + 1 < line))
            def _():
                sum_up(c, at).wait_send()

            @pl.when(jnp.logical_and(at < z, z >= 1))
            def _():
                sum_down(c, at).wait_send()

        return carry

    lax.fori_loop(0, chunks, drain, 0)


def land_kernel(att, dq, kv, gate, att_out, dq_out, dk_out, dv_out, gate_out):
    att_out[0] = att[...]
    dq_out[0] = dq[...]
    dk_out[0] = kv[0]
    dv_out[0] = kv[1]
    gate_out[...] = gate[:1, : gate_out.shape[1]]


def land(parts, head_count):
    att, dq, kv, gate = parts
    (toks, width), caps = att.shape, kv.shape[1]
    steps = max(1, width // 1024)
    cw = width // steps
    rows = pl.BlockSpec((toks, cw), lambda i: (0, i))
    pieces = pl.BlockSpec((2, caps, cw), lambda i: (0, 0, i))
    token = pl.BlockSpec((1, toks, cw), lambda i: (0, 0, i))
    cap = pl.BlockSpec((1, caps, cw), lambda i: (0, 0, i))
    out = pl.pallas_call(
        land_kernel,
        grid=(steps,),
        out_shape=(
            jax.ShapeDtypeStruct((1, toks, width), att.dtype),
            jax.ShapeDtypeStruct((1, toks, width), dq.dtype),
            jax.ShapeDtypeStruct((1, caps, width), kv.dtype),
            jax.ShapeDtypeStruct((1, caps, width), kv.dtype),
            jax.ShapeDtypeStruct((1, head_count), gate.dtype),
        ),
        in_specs=[rows, rows, pieces, pl.BlockSpec(gate.shape, lambda i: (0, 0))],
        out_specs=(token, token, cap, cap, pl.BlockSpec((1, head_count), lambda i: (0, 0))),
        compiler_params=pltpu.CompilerParams(vmem_limit_bytes=VMEM_LIMIT),
    )(att, dq, kv, gate)
    return (*out[:4], out[4][0])


def per_device(mesh_shape, video_queries, caption_keys, caption_values, out_grad, head_gate, video_len, cap_len):
    n, dp_n, grp_n = mesh_shape["seq"], mesh_shape["dp"], mesh_shape["grp"]
    toks, width = video_queries.shape[1:]
    caps = caption_keys.shape[1]
    head_count = head_gate.shape[0]
    heads = head_count // grp_n
    pair = 2 if n % 2 == 0 and heads % 2 == 0 else 1
    line = n // pair
    own_heads = heads // pair
    chunks = own_heads // 2 if own_heads % 2 == 0 else own_heads
    cw = width // pair // chunks
    lanes = -(-head_count // LANES) * LANES
    low = jnp.bfloat16
    any_spec = pl.BlockSpec(memory_space=pl.ANY)
    hbm = pl.BlockSpec(memory_space=pltpu.MemorySpace.HBM)
    smem = pl.BlockSpec(memory_space=pltpu.SMEM)
    vmem = pl.BlockSpec(memory_space=pltpu.VMEM)
    rows = pltpu.VMEM((chunks, pair, toks, cw), low)
    caption = pltpu.VMEM((chunks, n, 2, caps, cw), low)
    dma = pltpu.SemaphoreType.DMA
    out = pl.pallas_call(
        functools.partial(kernel, (n, pair, dp_n, grp_n, heads)),
        out_shape=(
            jax.ShapeDtypeStruct((toks, width), low),
            jax.ShapeDtypeStruct((toks, width), low),
            jax.ShapeDtypeStruct((2, caps, width), low),
            jax.ShapeDtypeStruct((8, lanes), jnp.float32),
        ),
        in_specs=[smem, smem, smem, hbm, hbm, hbm, hbm],
        out_specs=(any_spec, any_spec, any_spec, vmem),
        scratch_shapes=[
            rows,
            rows,
            caption,
            rows,
            rows,
            caption,
            caption,
            caption,
            pltpu.VMEM((n, 8, lanes), jnp.float32),
            pltpu.VMEM((dp_n * grp_n, 8, lanes), jnp.float32),
            pltpu.VMEM((8, lanes), jnp.float32),
            dma((chunks,)),
            dma((2, chunks)),
            dma((4,)),
            dma((2, line, chunks)),
            dma((2, line, chunks)),
            dma((2, line, chunks)),
            dma((2, line, chunks)),
            dma((3,)),
            dma((3,)),
            dma((2,)),
            dma((2,)),
        ],
        compiler_params=pltpu.CompilerParams(
            collective_id=0, has_side_effects=True, vmem_limit_bytes=VMEM_LIMIT
        ),
    )(
        head_gate,
        video_len,
        cap_len,
        video_queries[0],
        caption_keys[0],
        caption_values[0],
        out_grad[0],
    )
    return land(out, head_count)


def solution(mesh):
    rows = P("dp", "seq", "grp")
    return jax.shard_map(
        functools.partial(per_device, dict(mesh.shape)),
        mesh=mesh,
        in_specs=(rows, rows, rows, rows, P(), P("dp"), P("dp")),
        out_specs=(rows, rows, rows, rows, P()),
        check_vma=False,
    )
```

```python
import functools

import jax
import jax.numpy as jnp
from jax import lax
from jax.experimental import pallas as pl
from jax.experimental.pallas import tpu as pltpu
from jax.sharding import PartitionSpec as P

MESH = pl.DeviceIdType.MESH
LANES = 128
VMEM_LIMIT = 63 << 20
LAND_LIMIT = 63 << 20


def kernel(
    dims,
    gate_ref,
    vlen_ref,
    clen_ref,
    q_ref,
    k_ref,
    v_ref,
    g_ref,
    att_out,
    dq_out,
    kv_out,
    gate_out,
    qbuf,
    gbuf,
    kvbuf,
    obuf,
    dqbuf,
    part,
    part_up,
    part_down,
    gate_seq,
    gate_all,
    gate_mine,
    kv_recv,
    row_recv,
    pair_send,
    hop_recv,
    hop_send,
    sum_recv,
    sum_send,
    out_recv,
    out_send,
    gate_recv,
    gate_send,
):
    n, pair, dp_n, grp_n, heads = dims
    line = n // pair
    chunks, _, toks, cw = qbuf.shape
    caps = kvbuf.shape[3]
    cols = q_ref.shape[1] // pair
    hd = q_ref.shape[1] // heads
    per_chunk = cw // hd
    total_j = n * caps
    total_t = pair * toks
    peers = dp_n * grp_n
    lags = [0] + [s + 1 for s in range(1, line)]
    lag = lags[-1]

    me = lax.axis_index("seq")
    dp_me = lax.axis_index("dp")
    grp_me = lax.axis_index("grp")
    z = me // pair
    x = lax.rem(me, pair)
    side = dp_me * grp_n + grp_me

    barrier = pltpu.get_barrier_semaphore()
    for d in range(1, n):
        pl.semaphore_signal(
            barrier, inc=1, device_id={"seq": lax.rem(me + d, n)}, device_id_type=MESH
        )

    def side_id(d):
        other = lax.rem(side + d, peers)
        return {"dp": other // grp_n, "grp": lax.rem(other, grp_n)}

    def greet(d, carry):
        pl.semaphore_signal(barrier, inc=1, device_id=side_id(d), device_id_type=MESH)
        return carry

    lax.fori_loop(1, peers, greet, 0)
    pl.semaphore_wait(barrier, n - 1 + peers - 1)

    def columns(owner, c):
        return pl.ds(pl.multiple_of(owner * cols + c * cw, LANES), cw)

    def remote(src, dst, send, recv, seq):
        return pltpu.make_async_remote_copy(
            src_ref=src,
            dst_ref=dst,
            send_sem=send,
            recv_sem=recv,
            device_id={"seq": seq},
            device_id_type=MESH,
        )

    def slots(at):
        return pl.ds(at * pair, pair)

    def settle(ref, sem):
        pltpu.make_async_copy(ref, ref, sem).wait()

    def pair_inputs(c, carry):
        pieces = (
            (k_ref, kvbuf.at[c, me, 0], kv_recv.at[c]),
            (v_ref, kvbuf.at[c, me, 1], kv_recv.at[c]),
            (q_ref, qbuf.at[c, x], row_recv.at[0, c]),
            (g_ref, gbuf.at[c, x], row_recv.at[1, c]),
        )
        for d in range(1, pair):
            other = lax.rem(x + d, pair)
            for kind, (src, dst, sem) in enumerate(pieces):
                remote(
                    src.at[:, columns(other, c)], dst, pair_send.at[kind], sem, z * pair + other
                ).start()
        for src, dst, sem in pieces:
            pltpu.make_async_copy(src.at[:, columns(x, c)], dst, sem).start()
        return carry

    lax.fori_loop(0, chunks, pair_inputs, 0)

    gate_mine[...] = jnp.zeros_like(gate_mine)
    cap_len = clen_ref[0]
    video_len = vlen_ref[0]
    scale = hd ** (-0.5)
    lane = lax.broadcasted_iota(jnp.int32, gate_mine.shape, 1)

    def hop_up(c, s):
        block = kvbuf.at[c, slots(z - s)]
        return remote(block, block, hop_send.at[0, s, c], hop_recv.at[0, s + 1, c], me + pair)

    def hop_down(c, s):
        block = kvbuf.at[c, slots(z + s)]
        return remote(block, block, hop_send.at[1, s, c], hop_recv.at[1, s + 1, c], me - pair)

    def goes_up(s):
        return jnp.logical_and(z - s >= 0, z + 1 < line)

    def goes_down(s):
        return jnp.logical_and(z + s < line, z >= 1)

    def relay(c, s):
        if s == 0:
            settle(kvbuf.at[c, slots(z)], kv_recv.at[c])
        else:

            @pl.when(z - s >= 0)
            def _():
                settle(kvbuf.at[c, slots(z - s)], hop_recv.at[0, s, c])

            @pl.when(z + s < line)
            def _():
                settle(kvbuf.at[c, slots(z + s)], hop_recv.at[1, s, c])

        if s < line - 1:

            @pl.when(goes_up(s))
            def _():
                hop_up(c, s).start()

            @pl.when(goes_down(s))
            def _():
                hop_down(c, s).start()

    def transposed(a, b, left, right):
        return lax.dot_general(
            a, b, (((left,), (right,)), ((), ())), preferred_element_type=jnp.float32
        )

    def attend(c):
        settle(qbuf.at[c], row_recv.at[0, c])
        settle(gbuf.at[c], row_recv.at[1, c])
        for h in range(per_chunk):
            at = slice(h * hd, (h + 1) * hd)
            head = grp_me * heads + x * (heads // pair) + c * per_chunk + h
            gate = gate_ref[head]
            keys = kvbuf[c, :, 0, :, at].reshape(total_j, hd)
            values = kvbuf[c, :, 1, :, at].reshape(total_j, hd)
            queries = qbuf[c, :, :, at].reshape(total_t, hd)
            cot = gbuf[c, :, :, at].reshape(total_t, hd).astype(jnp.float32)
            key_live = lax.broadcasted_iota(jnp.int32, (total_j, total_t), 0) < cap_len
            scores = transposed(keys, queries, 1, 1) * scale
            scores = jnp.where(key_live, scores, -jnp.inf)
            shifted = jnp.exp(scores - jnp.max(scores, axis=0, keepdims=True))
            weights = shifted * (1.0 / jnp.sum(shifted, axis=0, keepdims=True))
            low = weights.astype(jnp.bfloat16)
            attention = transposed(values, low, 0, 0).T
            row = z * total_t + lax.broadcasted_iota(jnp.int32, (total_t, hd), 0)
            live = (row < video_len).astype(jnp.float32)
            obuf[c, :, :, at] = (
                (attention * gate * live).astype(jnp.bfloat16).reshape(pair, toks, hd)
            )
            gate_sum = jnp.sum(cot * attention * live, axis=0, keepdims=True)
            grad = (cot * gate * live).astype(jnp.bfloat16)
            gw = transposed(values, grad, 1, 1)
            delta = jnp.sum(weights * gw, axis=0, keepdims=True)
            gs = (weights * (gw - delta) * scale).astype(jnp.bfloat16)
            dq = transposed(keys, gs, 0, 0).T
            dqbuf[c, :, :, at] = dq.astype(jnp.bfloat16).reshape(pair, toks, hd)
            dk = jnp.dot(gs, queries, preferred_element_type=jnp.float32)
            dv = jnp.dot(low, grad, preferred_element_type=jnp.float32)
            part[c, :, 0, :, at] = dk.astype(jnp.bfloat16).reshape(n, caps, hd)
            part[c, :, 1, :, at] = dv.astype(jnp.bfloat16).reshape(n, caps, hd)
            gate_mine[...] += jnp.where(
                lane == head, jnp.sum(gate_sum, axis=1, keepdims=True), 0.0
            )
        mine = columns(x, c)
        for kind, (src, dst) in enumerate(((obuf, att_out), (dqbuf, dq_out))):
            for d in range(1, pair):
                other = lax.rem(x + d, pair)
                remote(
                    src.at[c, other],
                    dst.at[:, mine],
                    out_send.at[kind],
                    out_recv.at[kind],
                    z * pair + other,
                ).start()
            pltpu.make_async_copy(src.at[c, x], dst.at[:, mine], out_recv.at[kind]).start()

    def gather(c, at, way, source):
        settle(source.at[c, slots(at)], sum_recv.at[way, at, c])
        both = part[c, slots(at)].astype(jnp.float32) + source[c, slots(at)].astype(jnp.float32)
        part[c, slots(at)] = both.astype(jnp.bfloat16)

    def sum_up(c, at):
        return remote(
            part.at[c, slots(at)],
            part_up.at[c, slots(at)],
            sum_send.at[0, at, c],
            sum_recv.at[0, at, c],
            me + pair,
        )

    def sum_down(c, at):
        return remote(
            part.at[c, slots(at)],
            part_down.at[c, slots(at)],
            sum_send.at[1, at, c],
            sum_recv.at[1, at, c],
            me - pair,
        )

    def chain_up(c):
        for at in range(line - 1, 0, -1):

            @pl.when(at > z)
            def _():
                @pl.when(z > 0)
                def _():
                    gather(c, at, 0, part_up)

                sum_up(c, at).start()

    def chain_down(c):
        for at in range(line - 1):

            @pl.when(at < z)
            def _():
                @pl.when(z < line - 1)
                def _():
                    gather(c, at, 1, part_down)

                sum_down(c, at).start()

    def finish(c):
        @pl.when(z > 0)
        def _():
            gather(c, z, 0, part_up)

        @pl.when(z < line - 1)
        def _():
            gather(c, z, 1, part_down)

        mine = columns(x, c)
        for d in range(1, pair):
            other = lax.rem(x + d, pair)
            remote(
                part.at[c, z * pair + other],
                kv_out.at[:, :, mine],
                out_send.at[2],
                out_recv.at[2],
                z * pair + other,
            ).start()
        pltpu.make_async_copy(part.at[c, me], kv_out.at[:, :, mine], out_recv.at[2]).start()

    def within(c, run):
        @pl.when(jnp.logical_and(c >= 0, c < chunks))
        def _():
            run(c)

    def seq_id(d):
        return {"seq": lax.rem(me + d, n)}

    def start_gate(src, dst, count, slot, stage, target):
        pltpu.make_async_copy(src, dst.at[slot], gate_recv.at[stage]).start()

        def go(d, carry):
            pltpu.make_async_remote_copy(
                src_ref=src,
                dst_ref=dst.at[slot],
                send_sem=gate_send.at[stage],
                recv_sem=gate_recv.at[stage],
                device_id=target(d),
                device_id_type=MESH,
            ).start()
            return carry

        lax.fori_loop(1, count, go, 0)

    def end_gate(dst, count, stage):
        settle(dst, gate_recv.at[stage])
        if count > 1:
            settle(dst.at[pl.ds(0, count - 1)], gate_send.at[stage])

    def step(i, carry):
        for s in reversed(range(line)):
            within(i - lags[s], functools.partial(relay, s=s))
        within(i - lag, attend)

        @pl.when(i - lag == chunks - 1)
        def _():
            start_gate(gate_mine, gate_seq, n, me, 0, seq_id)

        within(i - lag - 2 * z, chain_up)
        within(i - lag - 2 * (line - 1 - z), chain_down)
        within(i - lag - 2 * (line - 1), finish)
        return carry


    lax.fori_loop(0, chunks + lag + 2 * (line - 1), step, 0)

    end_gate(gate_seq, n, 0)
    gate_mine[...] = jnp.sum(gate_seq[...], axis=0)
    start_gate(gate_mine, gate_all, peers, side, 1, side_id)
    end_gate(gate_all, peers, 1)
    gate_out[...] = jnp.sum(gate_all[...], axis=0)

    for kind, ref in enumerate((att_out, dq_out, kv_out)):
        settle(ref, out_recv.at[kind])
    if pair > 1:
        for kind in range(2):
            settle(kvbuf.at[:, pl.ds(0, pair - 1), 0], pair_send.at[kind])
            settle(qbuf.at[:, pl.ds(0, pair - 1)], pair_send.at[2 + kind])
            settle(obuf.at[:, pl.ds(0, pair - 1)], out_send.at[kind])
        settle(kvbuf.at[:, pl.ds(0, pair - 1)], out_send.at[2])

    def drain(c, carry):
        for s in range(line - 1):

            @pl.when(goes_up(s))
            def _():
                hop_up(c, s).wait_send()

            @pl.when(goes_down(s))
            def _():
                hop_down(c, s).wait_send()

        for at in range(line):

            @pl.when(jnp.logical_and(at > z, z + 1 < line))
            def _():
                sum_up(c, at).wait_send()

            @pl.when(jnp.logical_and(at < z, z >= 1))
            def _():
                sum_down(c, at).wait_send()

        return carry

    lax.fori_loop(0, chunks, drain, 0)


def land_kernel(att, dq, kv, gate, att_out, dq_out, dk_out, dv_out, gate_out):
    att_out[0] = att[...]
    dq_out[0] = dq[...]
    dk_out[0] = kv[0]
    dv_out[0] = kv[1]
    gate_out[...] = gate[:1, : gate_out.shape[1]]


def land(parts, head_count):
    att, dq, kv, gate = parts
    (toks, width), caps = att.shape, kv.shape[1]
    steps = max(1, width // 1024)
    cw = width // steps
    rows = pl.BlockSpec((toks, cw), lambda i: (0, i))
    pieces = pl.BlockSpec((2, caps, cw), lambda i: (0, 0, i))
    token = pl.BlockSpec((1, toks, cw), lambda i: (0, 0, i))
    cap = pl.BlockSpec((1, caps, cw), lambda i: (0, 0, i))
    out = pl.pallas_call(
        land_kernel,
        grid=(steps,),
        out_shape=(
            jax.ShapeDtypeStruct((1, toks, width), att.dtype),
            jax.ShapeDtypeStruct((1, toks, width), dq.dtype),
            jax.ShapeDtypeStruct((1, caps, width), kv.dtype),
            jax.ShapeDtypeStruct((1, caps, width), kv.dtype),
            jax.ShapeDtypeStruct((1, head_count), gate.dtype),
        ),
        in_specs=[rows, rows, pieces, pl.BlockSpec(gate.shape, lambda i: (0, 0))],
        out_specs=(token, token, cap, cap, pl.BlockSpec((1, head_count), lambda i: (0, 0))),
        compiler_params=pltpu.CompilerParams(vmem_limit_bytes=LAND_LIMIT),
    )(att, dq, kv, gate)
    return (*out[:4], out[4][0])


def per_device(mesh_shape, video_queries, caption_keys, caption_values, out_grad, head_gate, video_len, cap_len):
    n, dp_n, grp_n = mesh_shape["seq"], mesh_shape["dp"], mesh_shape["grp"]
    toks, width = video_queries.shape[1:]
    caps = caption_keys.shape[1]
    head_count = head_gate.shape[0]
    heads = head_count // grp_n
    pair = 2 if n % 2 == 0 and heads % 2 == 0 else 1
    line = n // pair
    own_heads = heads // pair
    chunks = own_heads // 2 if own_heads % 2 == 0 else own_heads
    cw = width // pair // chunks
    lanes = -(-head_count // LANES) * LANES
    low = jnp.bfloat16
    any_spec = pl.BlockSpec(memory_space=pl.ANY)
    hbm = pl.BlockSpec(memory_space=pltpu.MemorySpace.HBM)
    smem = pl.BlockSpec(memory_space=pltpu.SMEM)
    vmem = pl.BlockSpec(memory_space=pltpu.VMEM)
    rows = pltpu.VMEM((chunks, pair, toks, cw), low)
    caption = pltpu.VMEM((chunks, n, 2, caps, cw), low)
    dma = pltpu.SemaphoreType.DMA
    out = pl.pallas_call(
        functools.partial(kernel, (n, pair, dp_n, grp_n, heads)),
        out_shape=(
            jax.ShapeDtypeStruct((toks, width), low),
            jax.ShapeDtypeStruct((toks, width), low),
            jax.ShapeDtypeStruct((2, caps, width), low),
            jax.ShapeDtypeStruct((8, lanes), jnp.float32),
        ),
        in_specs=[smem, smem, smem, hbm, hbm, hbm, hbm],
        out_specs=(any_spec, any_spec, any_spec, vmem),
        scratch_shapes=[
            rows,
            rows,
            caption,
            rows,
            rows,
            caption,
            caption,
            caption,
            pltpu.VMEM((n, 8, lanes), jnp.float32),
            pltpu.VMEM((dp_n * grp_n, 8, lanes), jnp.float32),
            pltpu.VMEM((8, lanes), jnp.float32),
            dma((chunks,)),
            dma((2, chunks)),
            dma((4,)),
            dma((2, line, chunks)),
            dma((2, line, chunks)),
            dma((2, line, chunks)),
            dma((2, line, chunks)),
            dma((3,)),
            dma((3,)),
            dma((2,)),
            dma((2,)),
        ],
        compiler_params=pltpu.CompilerParams(
            collective_id=0, has_side_effects=True, vmem_limit_bytes=VMEM_LIMIT
        ),
    )(
        head_gate,
        video_len,
        cap_len,
        video_queries[0],
        caption_keys[0],
        caption_values[0],
        out_grad[0],
    )
    return land(out, head_count)


def solution(mesh):
    rows = P("dp", "seq", "grp")
    return jax.shard_map(
        functools.partial(per_device, dict(mesh.shape)),
        mesh=mesh,
        in_specs=(rows, rows, rows, rows, P(), P("dp"), P("dp")),
        out_specs=(rows, rows, rows, rows, P()),
        check_vma=False,
    )
```

```python
import functools

import jax
import jax.numpy as jnp
from jax import lax
from jax.experimental import pallas as pl
from jax.experimental.pallas import tpu as pltpu
from jax.sharding import PartitionSpec as P

MESH = pl.DeviceIdType.MESH
LANES = 128
VMEM_LIMIT = 63 << 20
LAND_LIMIT = 63 << 20


def kernel(
    dims,
    gate_ref,
    vlen_ref,
    clen_ref,
    q_ref,
    k_ref,
    v_ref,
    g_ref,
    att_out,
    dq_out,
    kv_out,
    gate_out,
    qbuf,
    gbuf,
    kvbuf,
    obuf,
    dqbuf,
    part,
    part_up,
    part_down,
    gate_seq,
    gate_all,
    gate_mine,
    kv_recv,
    row_recv,
    pair_send,
    hop_recv,
    hop_send,
    sum_recv,
    sum_send,
    out_recv,
    out_send,
    gate_recv,
    gate_send,
):
    n, pair, dp_n, grp_n, heads = dims
    line = n // pair
    chunks, _, toks, cw = qbuf.shape
    caps = kvbuf.shape[3]
    cols = q_ref.shape[1] // pair
    hd = q_ref.shape[1] // heads
    per_chunk = cw // hd
    total_j = n * caps
    total_t = pair * toks
    peers = dp_n * grp_n
    lags = [0] + [s + 1 for s in range(1, line)]
    lag = lags[-1]

    me = lax.axis_index("seq")
    dp_me = lax.axis_index("dp")
    grp_me = lax.axis_index("grp")
    z = me // pair
    x = lax.rem(me, pair)
    side = dp_me * grp_n + grp_me

    barrier = pltpu.get_barrier_semaphore()
    for d in range(1, n):
        pl.semaphore_signal(
            barrier, inc=1, device_id={"seq": lax.rem(me + d, n)}, device_id_type=MESH
        )

    def side_id(d):
        other = lax.rem(side + d, peers)
        return {"dp": other // grp_n, "grp": lax.rem(other, grp_n)}

    def greet(d, carry):
        pl.semaphore_signal(barrier, inc=1, device_id=side_id(d), device_id_type=MESH)
        return carry

    lax.fori_loop(1, peers, greet, 0)
    pl.semaphore_wait(barrier, n - 1 + peers - 1)

    def columns(owner, c):
        return pl.ds(pl.multiple_of(owner * cols + c * cw, LANES), cw)

    def remote(src, dst, send, recv, seq):
        return pltpu.make_async_remote_copy(
            src_ref=src,
            dst_ref=dst,
            send_sem=send,
            recv_sem=recv,
            device_id={"seq": seq},
            device_id_type=MESH,
        )

    def slots(at):
        return pl.ds(at * pair, pair)

    def settle(ref, sem):
        pltpu.make_async_copy(ref, ref, sem).wait()

    def pair_inputs(c, carry):
        pieces = (
            (k_ref, kvbuf.at[c, me, 0], kv_recv.at[c]),
            (v_ref, kvbuf.at[c, me, 1], kv_recv.at[c]),
            (q_ref, qbuf.at[c, x], row_recv.at[0, c]),
            (g_ref, gbuf.at[c, x], row_recv.at[1, c]),
        )
        for d in range(1, pair):
            other = lax.rem(x + d, pair)
            for kind, (src, dst, sem) in enumerate(pieces):
                remote(
                    src.at[:, columns(other, c)], dst, pair_send.at[kind], sem, z * pair + other
                ).start()
        for src, dst, sem in pieces:
            pltpu.make_async_copy(src.at[:, columns(x, c)], dst, sem).start()
        return carry

    lax.fori_loop(0, chunks, pair_inputs, 0)

    gate_mine[...] = jnp.zeros_like(gate_mine)
    cap_len = clen_ref[0]
    video_len = vlen_ref[0]
    scale = hd ** (-0.5)
    lane = lax.broadcasted_iota(jnp.int32, gate_mine.shape, 1)

    def hop_up(c, s):
        block = kvbuf.at[c, slots(z - s)]
        return remote(block, block, hop_send.at[0, s, c], hop_recv.at[0, s + 1, c], me + pair)

    def hop_down(c, s):
        block = kvbuf.at[c, slots(z + s)]
        return remote(block, block, hop_send.at[1, s, c], hop_recv.at[1, s + 1, c], me - pair)

    def goes_up(s):
        return jnp.logical_and(z - s >= 0, z + 1 < line)

    def goes_down(s):
        return jnp.logical_and(z + s < line, z >= 1)

    def relay(c, s):
        if s == 0:
            settle(kvbuf.at[c, slots(z)], kv_recv.at[c])
        else:

            @pl.when(z - s >= 0)
            def _():
                settle(kvbuf.at[c, slots(z - s)], hop_recv.at[0, s, c])

            @pl.when(z + s < line)
            def _():
                settle(kvbuf.at[c, slots(z + s)], hop_recv.at[1, s, c])

        if s < line - 1:

            @pl.when(goes_up(s))
            def _():
                hop_up(c, s).start()

            @pl.when(goes_down(s))
            def _():
                hop_down(c, s).start()

    def transposed(a, b, left, right):
        return lax.dot_general(
            a, b, (((left,), (right,)), ((), ())), preferred_element_type=jnp.float32
        )

    def attend(c):
        settle(qbuf.at[c], row_recv.at[0, c])
        settle(gbuf.at[c], row_recv.at[1, c])
        for h in range(per_chunk):
            at = slice(h * hd, (h + 1) * hd)
            head = grp_me * heads + x * (heads // pair) + c * per_chunk + h
            gate = gate_ref[head]
            keys = kvbuf[c, :, 0, :, at].reshape(total_j, hd)
            values = kvbuf[c, :, 1, :, at].reshape(total_j, hd)
            queries = qbuf[c, :, :, at].reshape(total_t, hd)
            cot = gbuf[c, :, :, at].reshape(total_t, hd).astype(jnp.float32)
            key_live = lax.broadcasted_iota(jnp.int32, (total_j, total_t), 0) < cap_len
            scores = transposed(keys, queries, 1, 1) * scale
            scores = jnp.where(key_live, scores, -jnp.inf)
            shifted = jnp.exp(scores - jnp.max(scores, axis=0, keepdims=True))
            weights = shifted * (1.0 / jnp.sum(shifted, axis=0, keepdims=True))
            low = weights.astype(jnp.bfloat16)
            attention = transposed(values, low, 0, 0).T
            row = z * total_t + lax.broadcasted_iota(jnp.int32, (total_t, hd), 0)
            live = (row < video_len).astype(jnp.float32)
            obuf[c, :, :, at] = (
                (attention * gate * live).astype(jnp.bfloat16).reshape(pair, toks, hd)
            )
            gate_sum = jnp.sum(cot * attention * live, axis=0, keepdims=True)
            grad = (cot * gate * live).astype(jnp.bfloat16)
            gw = transposed(values, grad, 1, 1)
            delta = jnp.sum(weights * gw, axis=0, keepdims=True)
            gs = (weights * (gw - delta) * scale).astype(jnp.bfloat16)
            dq = transposed(keys, gs, 0, 0).T
            dqbuf[c, :, :, at] = dq.astype(jnp.bfloat16).reshape(pair, toks, hd)
            dk = jnp.dot(gs, queries, preferred_element_type=jnp.float32)
            dv = jnp.dot(low, grad, preferred_element_type=jnp.float32)
            part[c, :, 0, :, at] = dk.astype(jnp.bfloat16).reshape(n, caps, hd)
            part[c, :, 1, :, at] = dv.astype(jnp.bfloat16).reshape(n, caps, hd)
            gate_mine[...] += jnp.where(
                lane == head, jnp.sum(gate_sum, axis=1, keepdims=True), 0.0
            )
        mine = columns(x, c)
        for kind, (src, dst) in enumerate(((obuf, att_out), (dqbuf, dq_out))):
            for d in range(1, pair):
                other = lax.rem(x + d, pair)
                remote(
                    src.at[c, other],
                    dst.at[:, mine],
                    out_send.at[kind],
                    out_recv.at[kind],
                    z * pair + other,
                ).start()
            pltpu.make_async_copy(src.at[c, x], dst.at[:, mine], out_recv.at[kind]).start()

    def gather(c, at, way, source):
        settle(source.at[c, slots(at)], sum_recv.at[way, at, c])
        both = part[c, slots(at)].astype(jnp.float32) + source[c, slots(at)].astype(jnp.float32)
        part[c, slots(at)] = both.astype(jnp.bfloat16)

    def sum_up(c, at):
        return remote(
            part.at[c, slots(at)],
            part_up.at[c, slots(at)],
            sum_send.at[0, at, c],
            sum_recv.at[0, at, c],
            me + pair,
        )

    def sum_down(c, at):
        return remote(
            part.at[c, slots(at)],
            part_down.at[c, slots(at)],
            sum_send.at[1, at, c],
            sum_recv.at[1, at, c],
            me - pair,
        )

    def chain_up(c):
        for at in range(line - 1, 0, -1):

            @pl.when(at > z)
            def _():
                @pl.when(z > 0)
                def _():
                    gather(c, at, 0, part_up)

                sum_up(c, at).start()

    def chain_down(c):
        for at in range(line - 1):

            @pl.when(at < z)
            def _():
                @pl.when(z < line - 1)
                def _():
                    gather(c, at, 1, part_down)

                sum_down(c, at).start()

    def finish(c):
        @pl.when(z > 0)
        def _():
            gather(c, z, 0, part_up)

        @pl.when(z < line - 1)
        def _():
            gather(c, z, 1, part_down)

        mine = columns(x, c)
        for d in range(1, pair):
            other = lax.rem(x + d, pair)
            remote(
                part.at[c, z * pair + other],
                kv_out.at[:, :, mine],
                out_send.at[2],
                out_recv.at[2],
                z * pair + other,
            ).start()
        pltpu.make_async_copy(part.at[c, me], kv_out.at[:, :, mine], out_recv.at[2]).start()

    def within(c, run):
        @pl.when(jnp.logical_and(c >= 0, c < chunks))
        def _():
            run(c)

    def seq_id(d):
        return {"seq": lax.rem(me + d, n)}

    def start_gate(src, dst, count, slot, stage, target):
        pltpu.make_async_copy(src, dst.at[slot], gate_recv.at[stage]).start()

        def go(d, carry):
            pltpu.make_async_remote_copy(
                src_ref=src,
                dst_ref=dst.at[slot],
                send_sem=gate_send.at[stage],
                recv_sem=gate_recv.at[stage],
                device_id=target(d),
                device_id_type=MESH,
            ).start()
            return carry

        lax.fori_loop(1, count, go, 0)

    def end_gate(dst, count, stage):
        settle(dst, gate_recv.at[stage])
        if count > 1:
            settle(dst.at[pl.ds(0, count - 1)], gate_send.at[stage])

    def step(i, carry):
        for s in reversed(range(line)):
            within(i - lags[s], functools.partial(relay, s=s))
        within(i - lag, attend)

        @pl.when(i - lag == chunks - 1)
        def _():
            start_gate(gate_mine, gate_seq, n, me, 0, seq_id)

        within(i - lag - 2 * z, chain_up)
        within(i - lag - 2 * (line - 1 - z), chain_down)
        within(i - lag - 2 * (line - 1), finish)
        return carry


    lax.fori_loop(0, chunks + lag + 2 * (line - 1), step, 0)

    end_gate(gate_seq, n, 0)
    gate_mine[...] = jnp.sum(gate_seq[...], axis=0)
    start_gate(gate_mine, gate_all, peers, side, 1, side_id)
    end_gate(gate_all, peers, 1)
    gate_out[...] = jnp.sum(gate_all[...], axis=0)

    for kind, ref in enumerate((att_out, dq_out, kv_out)):
        settle(ref, out_recv.at[kind])
    if pair > 1:
        for kind in range(2):
            settle(kvbuf.at[:, pl.ds(0, pair - 1), 0], pair_send.at[kind])
            settle(qbuf.at[:, pl.ds(0, pair - 1)], pair_send.at[2 + kind])
            settle(obuf.at[:, pl.ds(0, pair - 1)], out_send.at[kind])
        settle(kvbuf.at[:, pl.ds(0, pair - 1)], out_send.at[2])

    def drain(c, carry):
        for s in range(line - 1):

            @pl.when(goes_up(s))
            def _():
                hop_up(c, s).wait_send()

            @pl.when(goes_down(s))
            def _():
                hop_down(c, s).wait_send()

        for at in range(line):

            @pl.when(jnp.logical_and(at > z, z + 1 < line))
            def _():
                sum_up(c, at).wait_send()

            @pl.when(jnp.logical_and(at < z, z >= 1))
            def _():
                sum_down(c, at).wait_send()

        return carry

    lax.fori_loop(0, chunks, drain, 0)


def land_kernel(att, dq, kv, gate, att_out, dq_out, dk_out, dv_out, gate_out):
    att_out[0] = att[...]
    dq_out[0] = dq[...]
    dk_out[0] = kv[0]
    dv_out[0] = kv[1]
    gate_out[...] = gate[:1, : gate_out.shape[1]]


def land(parts, head_count):
    att, dq, kv, gate = parts
    (toks, width), caps = att.shape, kv.shape[1]
    steps = max(1, width // 1024)
    cw = width // steps
    rows = pl.BlockSpec((toks, cw), lambda i: (0, i))
    pieces = pl.BlockSpec((2, caps, cw), lambda i: (0, 0, i))
    token = pl.BlockSpec((1, toks, cw), lambda i: (0, 0, i))
    cap = pl.BlockSpec((1, caps, cw), lambda i: (0, 0, i))
    out = pl.pallas_call(
        land_kernel,
        grid=(steps,),
        out_shape=(
            jax.ShapeDtypeStruct((1, toks, width), att.dtype),
            jax.ShapeDtypeStruct((1, toks, width), dq.dtype),
            jax.ShapeDtypeStruct((1, caps, width), kv.dtype),
            jax.ShapeDtypeStruct((1, caps, width), kv.dtype),
            jax.ShapeDtypeStruct((1, head_count), gate.dtype),
        ),
        in_specs=[rows, rows, pieces, pl.BlockSpec(gate.shape, lambda i: (0, 0))],
        out_specs=(token, token, cap, cap, pl.BlockSpec((1, head_count), lambda i: (0, 0))),
        compiler_params=pltpu.CompilerParams(vmem_limit_bytes=LAND_LIMIT),
    )(att, dq, kv, gate)
    return (*out[:4], out[4][0])


def per_device(mesh_shape, video_queries, caption_keys, caption_values, out_grad, head_gate, video_len, cap_len):
    n, dp_n, grp_n = mesh_shape["seq"], mesh_shape["dp"], mesh_shape["grp"]
    toks, width = video_queries.shape[1:]
    caps = caption_keys.shape[1]
    head_count = head_gate.shape[0]
    heads = head_count // grp_n
    pair = 2 if n % 2 == 0 and heads % 2 == 0 else 1
    line = n // pair
    own_heads = heads // pair
    chunks = own_heads
    cw = width // pair // chunks
    lanes = -(-head_count // LANES) * LANES
    low = jnp.bfloat16
    any_spec = pl.BlockSpec(memory_space=pl.ANY)
    hbm = pl.BlockSpec(memory_space=pltpu.MemorySpace.HBM)
    smem = pl.BlockSpec(memory_space=pltpu.SMEM)
    vmem = pl.BlockSpec(memory_space=pltpu.VMEM)
    rows = pltpu.VMEM((chunks, pair, toks, cw), low)
    caption = pltpu.VMEM((chunks, n, 2, caps, cw), low)
    dma = pltpu.SemaphoreType.DMA
    out = pl.pallas_call(
        functools.partial(kernel, (n, pair, dp_n, grp_n, heads)),
        out_shape=(
            jax.ShapeDtypeStruct((toks, width), low),
            jax.ShapeDtypeStruct((toks, width), low),
            jax.ShapeDtypeStruct((2, caps, width), low),
            jax.ShapeDtypeStruct((8, lanes), jnp.float32),
        ),
        in_specs=[smem, smem, smem, hbm, hbm, hbm, hbm],
        out_specs=(any_spec, any_spec, any_spec, vmem),
        scratch_shapes=[
            rows,
            rows,
            caption,
            rows,
            rows,
            caption,
            caption,
            caption,
            pltpu.VMEM((n, 8, lanes), jnp.float32),
            pltpu.VMEM((dp_n * grp_n, 8, lanes), jnp.float32),
            pltpu.VMEM((8, lanes), jnp.float32),
            dma((chunks,)),
            dma((2, chunks)),
            dma((4,)),
            dma((2, line, chunks)),
            dma((2, line, chunks)),
            dma((2, line, chunks)),
            dma((2, line, chunks)),
            dma((3,)),
            dma((3,)),
            dma((2,)),
            dma((2,)),
        ],
        compiler_params=pltpu.CompilerParams(
            collective_id=0, has_side_effects=True, vmem_limit_bytes=VMEM_LIMIT
        ),
    )(
        head_gate,
        video_len,
        cap_len,
        video_queries[0],
        caption_keys[0],
        caption_values[0],
        out_grad[0],
    )
    return land(out, head_count)


def solution(mesh):
    rows = P("dp", "seq", "grp")
    return jax.shard_map(
        functools.partial(per_device, dict(mesh.shape)),
        mesh=mesh,
        in_specs=(rows, rows, rows, rows, P(), P("dp"), P("dp")),
        out_specs=(rows, rows, rows, rows, P()),
        check_vma=False,
    )
```

```python
import functools

import jax
import jax.numpy as jnp
from jax import lax
from jax.experimental import pallas as pl
from jax.experimental.pallas import tpu as pltpu
from jax.sharding import PartitionSpec as P

MESH = pl.DeviceIdType.MESH
LANES = 128
VMEM_LIMIT = 63 << 20
LAND_LIMIT = 63 << 20


def kernel(
    dims,
    gate_ref,
    vlen_ref,
    clen_ref,
    q_ref,
    k_ref,
    v_ref,
    g_ref,
    att_out,
    dq_out,
    kv_out,
    gate_out,
    qbuf,
    gbuf,
    kvbuf,
    obuf,
    dqbuf,
    part,
    part_up,
    part_down,
    gate_seq,
    gate_all,
    gate_mine,
    kv_recv,
    row_recv,
    pair_send,
    hop_recv,
    hop_send,
    sum_recv,
    sum_send,
    out_recv,
    out_send,
    gate_recv,
    gate_send,
):
    n, pair, dp_n, grp_n, heads = dims
    line = n // pair
    chunks, _, toks, cw = qbuf.shape
    caps = kvbuf.shape[3]
    cols = q_ref.shape[1] // pair
    hd = q_ref.shape[1] // heads
    per_chunk = cw // hd
    total_j = n * caps
    total_t = pair * toks
    peers = dp_n * grp_n
    lags = [2 * s for s in range(line)]
    lag = lags[-1]

    me = lax.axis_index("seq")
    dp_me = lax.axis_index("dp")
    grp_me = lax.axis_index("grp")
    z = me // pair
    x = lax.rem(me, pair)
    side = dp_me * grp_n + grp_me

    barrier = pltpu.get_barrier_semaphore()
    for d in range(1, n):
        pl.semaphore_signal(
            barrier, inc=1, device_id={"seq": lax.rem(me + d, n)}, device_id_type=MESH
        )

    def side_id(d):
        other = lax.rem(side + d, peers)
        return {"dp": other // grp_n, "grp": lax.rem(other, grp_n)}

    def greet(d, carry):
        pl.semaphore_signal(barrier, inc=1, device_id=side_id(d), device_id_type=MESH)
        return carry

    lax.fori_loop(1, peers, greet, 0)
    pl.semaphore_wait(barrier, n - 1 + peers - 1)

    def columns(owner, c):
        return pl.ds(pl.multiple_of(owner * cols + c * cw, LANES), cw)

    def remote(src, dst, send, recv, seq):
        return pltpu.make_async_remote_copy(
            src_ref=src,
            dst_ref=dst,
            send_sem=send,
            recv_sem=recv,
            device_id={"seq": seq},
            device_id_type=MESH,
        )

    def slots(at):
        return pl.ds(at * pair, pair)

    def settle(ref, sem):
        pltpu.make_async_copy(ref, ref, sem).wait()

    def pair_inputs(c, carry):
        pieces = (
            (k_ref, kvbuf.at[c, me, 0], kv_recv.at[c]),
            (v_ref, kvbuf.at[c, me, 1], kv_recv.at[c]),
            (q_ref, qbuf.at[c, x], row_recv.at[0, c]),
            (g_ref, gbuf.at[c, x], row_recv.at[1, c]),
        )
        for d in range(1, pair):
            other = lax.rem(x + d, pair)
            for kind, (src, dst, sem) in enumerate(pieces):
                remote(
                    src.at[:, columns(other, c)], dst, pair_send.at[kind], sem, z * pair + other
                ).start()
        for src, dst, sem in pieces:
            pltpu.make_async_copy(src.at[:, columns(x, c)], dst, sem).start()
        return carry

    lax.fori_loop(0, chunks, pair_inputs, 0)

    gate_mine[...] = jnp.zeros_like(gate_mine)
    cap_len = clen_ref[0]
    video_len = vlen_ref[0]
    scale = hd ** (-0.5)
    lane = lax.broadcasted_iota(jnp.int32, gate_mine.shape, 1)

    def hop_up(c, s):
        block = kvbuf.at[c, slots(z - s)]
        return remote(block, block, hop_send.at[0, s, c], hop_recv.at[0, s + 1, c], me + pair)

    def hop_down(c, s):
        block = kvbuf.at[c, slots(z + s)]
        return remote(block, block, hop_send.at[1, s, c], hop_recv.at[1, s + 1, c], me - pair)

    def goes_up(s):
        return jnp.logical_and(z - s >= 0, z + 1 < line)

    def goes_down(s):
        return jnp.logical_and(z + s < line, z >= 1)

    def relay(c, s):
        if s == 0:
            settle(kvbuf.at[c, slots(z)], kv_recv.at[c])
        else:

            @pl.when(z - s >= 0)
            def _():
                settle(kvbuf.at[c, slots(z - s)], hop_recv.at[0, s, c])

            @pl.when(z + s < line)
            def _():
                settle(kvbuf.at[c, slots(z + s)], hop_recv.at[1, s, c])

        if s < line - 1:

            @pl.when(goes_up(s))
            def _():
                hop_up(c, s).start()

            @pl.when(goes_down(s))
            def _():
                hop_down(c, s).start()

    def transposed(a, b, left, right):
        return lax.dot_general(
            a, b, (((left,), (right,)), ((), ())), preferred_element_type=jnp.float32
        )

    def attend(c):
        settle(qbuf.at[c], row_recv.at[0, c])
        settle(gbuf.at[c], row_recv.at[1, c])
        for h in range(per_chunk):
            at = slice(h * hd, (h + 1) * hd)
            head = grp_me * heads + x * (heads // pair) + c * per_chunk + h
            gate = gate_ref[head]
            keys = kvbuf[c, :, 0, :, at].reshape(total_j, hd)
            values = kvbuf[c, :, 1, :, at].reshape(total_j, hd)
            queries = qbuf[c, :, :, at].reshape(total_t, hd)
            cot = gbuf[c, :, :, at].reshape(total_t, hd).astype(jnp.float32)
            key_live = lax.broadcasted_iota(jnp.int32, (total_j, total_t), 0) < cap_len
            scores = transposed(keys, queries, 1, 1) * scale
            scores = jnp.where(key_live, scores, -jnp.inf)
            shifted = jnp.exp(scores - jnp.max(scores, axis=0, keepdims=True))
            weights = shifted * (1.0 / jnp.sum(shifted, axis=0, keepdims=True))
            low = weights.astype(jnp.bfloat16)
            attention = transposed(values, low, 0, 0).T
            row = z * total_t + lax.broadcasted_iota(jnp.int32, (total_t, hd), 0)
            live = (row < video_len).astype(jnp.float32)
            obuf[c, :, :, at] = (
                (attention * gate * live).astype(jnp.bfloat16).reshape(pair, toks, hd)
            )
            gate_sum = jnp.sum(cot * attention * live, axis=0, keepdims=True)
            grad = (cot * gate * live).astype(jnp.bfloat16)
            gw = transposed(values, grad, 1, 1)
            delta = jnp.sum(weights * gw, axis=0, keepdims=True)
            gs = (weights * (gw - delta) * scale).astype(jnp.bfloat16)
            dq = transposed(keys, gs, 0, 0).T
            dqbuf[c, :, :, at] = dq.astype(jnp.bfloat16).reshape(pair, toks, hd)
            dk = jnp.dot(gs, queries, preferred_element_type=jnp.float32)
            dv = jnp.dot(low, grad, preferred_element_type=jnp.float32)
            part[c, :, 0, :, at] = dk.astype(jnp.bfloat16).reshape(n, caps, hd)
            part[c, :, 1, :, at] = dv.astype(jnp.bfloat16).reshape(n, caps, hd)
            gate_mine[...] += jnp.where(
                lane == head, jnp.sum(gate_sum, axis=1, keepdims=True), 0.0
            )
        mine = columns(x, c)
        for kind, (src, dst) in enumerate(((obuf, att_out), (dqbuf, dq_out))):
            for d in range(1, pair):
                other = lax.rem(x + d, pair)
                remote(
                    src.at[c, other],
                    dst.at[:, mine],
                    out_send.at[kind],
                    out_recv.at[kind],
                    z * pair + other,
                ).start()
            pltpu.make_async_copy(src.at[c, x], dst.at[:, mine], out_recv.at[kind]).start()

    def gather(c, at, way, source):
        settle(source.at[c, slots(at)], sum_recv.at[way, at, c])
        both = part[c, slots(at)].astype(jnp.float32) + source[c, slots(at)].astype(jnp.float32)
        part[c, slots(at)] = both.astype(jnp.bfloat16)

    def sum_up(c, at):
        return remote(
            part.at[c, slots(at)],
            part_up.at[c, slots(at)],
            sum_send.at[0, at, c],
            sum_recv.at[0, at, c],
            me + pair,
        )

    def sum_down(c, at):
        return remote(
            part.at[c, slots(at)],
            part_down.at[c, slots(at)],
            sum_send.at[1, at, c],
            sum_recv.at[1, at, c],
            me - pair,
        )

    def chain_up(c):
        for at in range(line - 1, 0, -1):

            @pl.when(at > z)
            def _():
                @pl.when(z > 0)
                def _():
                    gather(c, at, 0, part_up)

                sum_up(c, at).start()

    def chain_down(c):
        for at in range(line - 1):

            @pl.when(at < z)
            def _():
                @pl.when(z < line - 1)
                def _():
                    gather(c, at, 1, part_down)

                sum_down(c, at).start()

    def finish(c):
        @pl.when(z > 0)
        def _():
            gather(c, z, 0, part_up)

        @pl.when(z < line - 1)
        def _():
            gather(c, z, 1, part_down)

        mine = columns(x, c)
        for d in range(1, pair):
            other = lax.rem(x + d, pair)
            remote(
                part.at[c, z * pair + other],
                kv_out.at[:, :, mine],
                out_send.at[2],
                out_recv.at[2],
                z * pair + other,
            ).start()
        pltpu.make_async_copy(part.at[c, me], kv_out.at[:, :, mine], out_recv.at[2]).start()

    def within(c, run):
        @pl.when(jnp.logical_and(c >= 0, c < chunks))
        def _():
            run(c)

    def seq_id(d):
        return {"seq": lax.rem(me + d, n)}

    def start_gate(src, dst, count, slot, stage, target):
        pltpu.make_async_copy(src, dst.at[slot], gate_recv.at[stage]).start()

        def go(d, carry):
            pltpu.make_async_remote_copy(
                src_ref=src,
                dst_ref=dst.at[slot],
                send_sem=gate_send.at[stage],
                recv_sem=gate_recv.at[stage],
                device_id=target(d),
                device_id_type=MESH,
            ).start()
            return carry

        lax.fori_loop(1, count, go, 0)

    def end_gate(dst, count, stage):
        settle(dst, gate_recv.at[stage])
        if count > 1:
            settle(dst.at[pl.ds(0, count - 1)], gate_send.at[stage])

    def step(i, carry):
        for s in reversed(range(line)):
            within(i - lags[s], functools.partial(relay, s=s))
        within(i - lag, attend)

        @pl.when(i - lag == chunks - 1)
        def _():
            start_gate(gate_mine, gate_seq, n, me, 0, seq_id)

        within(i - lag - 2 * z, chain_up)
        within(i - lag - 2 * (line - 1 - z), chain_down)
        within(i - lag - 2 * (line - 1), finish)
        return carry


    lax.fori_loop(0, chunks + lag + 2 * (line - 1), step, 0)

    end_gate(gate_seq, n, 0)
    gate_mine[...] = jnp.sum(gate_seq[...], axis=0)
    start_gate(gate_mine, gate_all, peers, side, 1, side_id)
    end_gate(gate_all, peers, 1)
    gate_out[...] = jnp.sum(gate_all[...], axis=0)

    for kind, ref in enumerate((att_out, dq_out, kv_out)):
        settle(ref, out_recv.at[kind])
    if pair > 1:
        for kind in range(2):
            settle(kvbuf.at[:, pl.ds(0, pair - 1), 0], pair_send.at[kind])
            settle(qbuf.at[:, pl.ds(0, pair - 1)], pair_send.at[2 + kind])
            settle(obuf.at[:, pl.ds(0, pair - 1)], out_send.at[kind])
        settle(kvbuf.at[:, pl.ds(0, pair - 1)], out_send.at[2])

    def drain(c, carry):
        for s in range(line - 1):

            @pl.when(goes_up(s))
            def _():
                hop_up(c, s).wait_send()

            @pl.when(goes_down(s))
            def _():
                hop_down(c, s).wait_send()

        for at in range(line):

            @pl.when(jnp.logical_and(at > z, z + 1 < line))
            def _():
                sum_up(c, at).wait_send()

            @pl.when(jnp.logical_and(at < z, z >= 1))
            def _():
                sum_down(c, at).wait_send()

        return carry

    lax.fori_loop(0, chunks, drain, 0)


def land_kernel(att, dq, kv, gate, att_out, dq_out, dk_out, dv_out, gate_out):
    att_out[0] = att[...]
    dq_out[0] = dq[...]
    dk_out[0] = kv[0]
    dv_out[0] = kv[1]
    gate_out[...] = gate[:1, : gate_out.shape[1]]


def land(parts, head_count):
    att, dq, kv, gate = parts
    (toks, width), caps = att.shape, kv.shape[1]
    steps = max(1, width // 1024)
    cw = width // steps
    rows = pl.BlockSpec((toks, cw), lambda i: (0, i))
    pieces = pl.BlockSpec((2, caps, cw), lambda i: (0, 0, i))
    token = pl.BlockSpec((1, toks, cw), lambda i: (0, 0, i))
    cap = pl.BlockSpec((1, caps, cw), lambda i: (0, 0, i))
    out = pl.pallas_call(
        land_kernel,
        grid=(steps,),
        out_shape=(
            jax.ShapeDtypeStruct((1, toks, width), att.dtype),
            jax.ShapeDtypeStruct((1, toks, width), dq.dtype),
            jax.ShapeDtypeStruct((1, caps, width), kv.dtype),
            jax.ShapeDtypeStruct((1, caps, width), kv.dtype),
            jax.ShapeDtypeStruct((1, head_count), gate.dtype),
        ),
        in_specs=[rows, rows, pieces, pl.BlockSpec(gate.shape, lambda i: (0, 0))],
        out_specs=(token, token, cap, cap, pl.BlockSpec((1, head_count), lambda i: (0, 0))),
        compiler_params=pltpu.CompilerParams(vmem_limit_bytes=LAND_LIMIT),
    )(att, dq, kv, gate)
    return (*out[:4], out[4][0])


def per_device(mesh_shape, video_queries, caption_keys, caption_values, out_grad, head_gate, video_len, cap_len):
    n, dp_n, grp_n = mesh_shape["seq"], mesh_shape["dp"], mesh_shape["grp"]
    toks, width = video_queries.shape[1:]
    caps = caption_keys.shape[1]
    head_count = head_gate.shape[0]
    heads = head_count // grp_n
    pair = 2 if n % 2 == 0 and heads % 2 == 0 else 1
    line = n // pair
    own_heads = heads // pair
    chunks = own_heads
    cw = width // pair // chunks
    lanes = -(-head_count // LANES) * LANES
    low = jnp.bfloat16
    any_spec = pl.BlockSpec(memory_space=pl.ANY)
    hbm = pl.BlockSpec(memory_space=pltpu.MemorySpace.HBM)
    smem = pl.BlockSpec(memory_space=pltpu.SMEM)
    vmem = pl.BlockSpec(memory_space=pltpu.VMEM)
    rows = pltpu.VMEM((chunks, pair, toks, cw), low)
    caption = pltpu.VMEM((chunks, n, 2, caps, cw), low)
    dma = pltpu.SemaphoreType.DMA
    out = pl.pallas_call(
        functools.partial(kernel, (n, pair, dp_n, grp_n, heads)),
        out_shape=(
            jax.ShapeDtypeStruct((toks, width), low),
            jax.ShapeDtypeStruct((toks, width), low),
            jax.ShapeDtypeStruct((2, caps, width), low),
            jax.ShapeDtypeStruct((8, lanes), jnp.float32),
        ),
        in_specs=[smem, smem, smem, hbm, hbm, hbm, hbm],
        out_specs=(any_spec, any_spec, any_spec, vmem),
        scratch_shapes=[
            rows,
            rows,
            caption,
            rows,
            rows,
            caption,
            caption,
            caption,
            pltpu.VMEM((n, 8, lanes), jnp.float32),
            pltpu.VMEM((dp_n * grp_n, 8, lanes), jnp.float32),
            pltpu.VMEM((8, lanes), jnp.float32),
            dma((chunks,)),
            dma((2, chunks)),
            dma((4,)),
            dma((2, line, chunks)),
            dma((2, line, chunks)),
            dma((2, line, chunks)),
            dma((2, line, chunks)),
            dma((3,)),
            dma((3,)),
            dma((2,)),
            dma((2,)),
        ],
        compiler_params=pltpu.CompilerParams(
            collective_id=0, has_side_effects=True, vmem_limit_bytes=VMEM_LIMIT
        ),
    )(
        head_gate,
        video_len,
        cap_len,
        video_queries[0],
        caption_keys[0],
        caption_values[0],
        out_grad[0],
    )
    return land(out, head_count)


def solution(mesh):
    rows = P("dp", "seq", "grp")
    return jax.shard_map(
        functools.partial(per_device, dict(mesh.shape)),
        mesh=mesh,
        in_specs=(rows, rows, rows, rows, P(), P("dp"), P("dp")),
        out_specs=(rows, rows, rows, rows, P()),
        check_vma=False,
    )
```
